256 devices in a mesh: expert: 32 (over x, z), dp: 8 (over y, core).
Axes of the slice: x: 4, y: 4, z: 8, core: 2. Of those that a mesh axis runs over, the one named last changes fastest.
Arguments:
- tokens: bfloat16 [32768, 2560], P(('expert', 'dp')), may hold values from -6 to 6
- routing: int32 [32768, 6], P(('expert', 'dp')), may hold values from 0 to 31, all different within a row; in each aligned block of 128 rows (0 to 127, 128 to 255, ...) at most 36 rows name the same one
- grad_up: bfloat16 [32, 9216, 768], P('expert', 'dp'), may hold values from -6 to 6
- up_shard: bfloat16 [32, 2560, 768], P('expert', 'dp'), may hold values from -0.125 to 0.125
- error_feedback: bfloat16 [32, 20480, 768], P('expert', 'dp'), may hold values from -60 to 60
- moment_one: bfloat16 [32, 2560, 768], P('expert', 'dp'), may hold values from -3 to 3
- moment_two: bfloat16 [32, 2560, 768], P('expert', 'dp'), may hold values from 0.049804688 to 0.796875
- loss_scale: float32 [], replicated, may hold values from 8 to 32
Outputs:
- grad_tokens: bfloat16 [32768, 2560], P(('expert', 'dp'))
- new_weights: bfloat16 [32, 2560, 768], P('expert')
- new_moment_one: bfloat16 [32, 2560, 768], P('expert', 'dp')
- new_moment_two: bfloat16 [32, 2560, 768], P('expert', 'dp')
The draws below stay inside these ranges and needn't reach their ends.
Inputs may be any that keep to these rules, and one draw needn't show every extreme that they name: `routing`: each row names 6 different experts; among the 128 rows of one device no expert is named more than 36 times, a bound that some block reaches.
All inputs are finite; a program needn't handle non-finite values.
Results may differ from the reference program's by a relative error of at most 0.0049.
Values may be sent and summed in bfloat16 or wider, within the bound.
No kernel may reach another device: no remote copies, remote signals or barrier semaphores. Data moves between devices by JAX's collectives and lax.ppermute only.
A program may use at most 128 MiB of HBM per device.

```python
import math
import jax
import jax.numpy as jnp
import numpy as np
from jax import lax

D = 2560
FF = 768
TOP = 6
QB = 128
STEP = 20
TOK_DEV = 128
EXPERTS = 32
CAP = 36
SLOTS = 9216
TOKENS = 32768
N_EXPERT = 32
N_DP = 8


def level_of(rng, extent, pieces, low, high):
    factor_of = 1.0
    for position, parts in pieces:
        heights = jax.random.uniform(jax.random.fold_in(jax.random.fold_in(rng, 6), position), (parts,), jnp.float32, low / len(pieces), high / len(pieces))
        factor_of = factor_of * jnp.repeat(jnp.exp(heights), extent[position] // parts).reshape((-1,) + (1,) * (len(extent) - 1 - position))
    return factor_of


def assign_block(key, own, number, rows, number_of, top, bound, skew):
    ranking = jax.random.permutation(key, number_of)
    crowded, usual = portions_of(number_of, rows * top, bound, skew, True), portions_of(number_of, rows * top, bound, skew, False)
    places = jnp.arange(number_of)

    def named(lengths, turn):
        used = int((lengths > 0).sum())
        fixed = max(1, used // 4)
        shifted = fixed + (places - fixed + turn * (used - fixed)) % max(1, number_of - fixed)
        return jnp.zeros((number_of,), jnp.int32).at[ranking[jnp.where(places < fixed, places, shifted)]].set(jnp.asarray(lengths, jnp.int32))

    lengths = jnp.where(number % 4 == 0, named(crowded, number // 4), named(usual, number - number // 4 - 1))
    mixed = jax.random.permutation(jax.random.fold_in(own, 3), number_of)
    giver, taker = mixed[0:number_of // 2 * 2:2], mixed[1:number_of // 2 * 2:2]
    slack = jnp.minimum(lengths[giver] - 1, bound - lengths[taker]) // 2
    slack = jnp.where((giver == ranking[0]) | (taker == ranking[0]) | (lengths[taker] == 0), 0, jnp.maximum(slack, 0))
    shifted = jax.random.randint(jax.random.fold_in(own, 4), (number_of // 2,), 0, 1 << 20) % (slack + 1)
    lengths = lengths.at[giver].add(-shifted).at[taker].add(shifted)
    members = jnp.searchsorted(jnp.cumsum(lengths), jnp.arange(rows * top), side="right").astype(jnp.int32)
    grid = members.reshape(top, rows).T
    grid = grid[jax.random.permutation(jax.random.fold_in(own, 1), rows)]
    turn = jax.random.randint(jax.random.fold_in(own, 2), (rows, 1), 0, top)
    return jnp.take_along_axis(grid, (jnp.arange(top)[None, :] + turn) % top, axis=1)


def portions_of(amount, total, reach, skew, full):
    weights = [(1 << 20) // math.isqrt(rank ** skew) + 1 for rank in range(1, amount + 1)]
    largest = reach if full else min(reach, max(-(-total // amount), total * weights[0] // sum(weights)))
    least = 1 if total - largest >= amount - 1 else 0
    given, rest = [largest] + [least] * (amount - 1), total - largest - least * (amount - 1)
    while rest > 0:
        candidates = [i for i in range(1, amount) if given[i] < largest] or [i for i in range(1, amount) if given[i] < reach]
        whole, remaining = sum([weights[i] for i in candidates]), rest
        for i in candidates:
            addition = min(reach - given[i], max(1, remaining * weights[i] // whole), rest)
            given[i] = given[i] + addition
            rest = rest - addition
    return np.array(given)


def scatter_about(own_key, dims, width, bound, shards=(), held_as=jnp.bfloat16):
    factor_of = level_of(own_key, dims, shards, -0.22, 0.18) if shards else 1.0
    drawn = jax.random.normal(own_key, dims, jnp.float32) * width * factor_of
    return jnp.minimum(jnp.maximum(drawn, -bound), bound).astype(held_as)


def setup_inputs(seed: int = 0) -> dict:
    keys = jax.random.split(jax.random.key(seed), 9)
    tokens = scatter_about(keys[0], (TOKENS, D), 1.0, 6.0, ((0, 256),))
    routing_keys = jax.random.split(jax.random.fold_in(keys[1], 1), TOKENS // TOK_DEV)
    routing_turns = jax.random.permutation(jax.random.fold_in(keys[1], 3), TOKENS // TOK_DEV)
    routing = jax.vmap(lambda own, number: assign_block(jax.random.fold_in(keys[1], 2), own, number, TOK_DEV, EXPERTS, TOP, CAP, 2))(routing_keys, routing_turns).reshape((TOKENS, TOP))
    grad_up = scatter_about(keys[2], (EXPERTS, SLOTS, FF), 1.0, 6.0, ((0, 32), (1, 8)))
    up_shard = scatter_about(keys[3], (EXPERTS, D, FF), D ** -0.5, 0.125, ((0, 32), (1, 8)))
    error_feedback = scatter_about(keys[4], (EXPERTS, N_DP * D, FF), 10.0, 60.0, ((0, 32), (1, 8)))
    moment_one = scatter_about(keys[5], (EXPERTS, D, FF), 0.5, 3.0, ((0, 32), (1, 8)))
    moment_two = jnp.clip(jnp.exp(math.log(0.796875) - 2.7725887 * jax.random.uniform(keys[6], (EXPERTS, D, FF), jnp.float32) ** level_of(keys[6], (EXPERTS, D, FF), ((0, 32), (1, 8)), -0.2, 0.2)), 0.049804688, 0.796875).astype(jnp.bfloat16)
    loss_scale = jnp.clip(jnp.exp(jax.random.uniform(keys[7], (), jnp.float32, math.log(8.0), math.log(32.0))), 8.0, 32.0)
    return {"tokens": tokens, "routing": routing, "grad_up": grad_up, "up_shard": up_shard, "error_feedback": error_feedback, "moment_one": moment_one, "moment_two": moment_two, "loss_scale": loss_scale}


learn_rate = 0.001
beta_one = 0.9
beta_two = 0.999
decay_rate = 0.1
adam_eps = 1e-08
quant_top = 127.0
amax_eps = 1e-06

def place_pairs(routes_block, expert_total):
    chosen = routes_block.reshape(-1)
    onehot = (chosen[:, None] == jnp.arange(expert_total, dtype=jnp.int32)[None, :]).astype(jnp.int32)
    before = jnp.cumsum(onehot, axis=0) - onehot
    within = lax.optimization_barrier(jnp.sum(before * onehot, axis=1)).astype(jnp.int32)
    counts = lax.optimization_barrier(jnp.sum(onehot, axis=0)).astype(jnp.int32)
    return (chosen, within, counts)

def dequantized(values):
    row_total, columns = values.shape
    blocks = values.reshape(row_total, columns // QB, QB)
    block_scale = ((lax.optimization_barrier(jnp.max(jnp.abs(blocks), axis=2)) + amax_eps) / quant_top).astype(jnp.bfloat16)
    levels = (blocks / block_scale.astype(jnp.float32)[:, :, None]).astype(jnp.bfloat16)
    return (levels, block_scale)

def adam_update(weights, first_moment, second_moment, gradient):
    first_new = beta_one * first_moment.astype(jnp.float32) + (1.0 - beta_one) * gradient
    second_new = beta_two * second_moment.astype(jnp.float32) + (1.0 - beta_two) * gradient * gradient
    first_hat = first_new / (1.0 - beta_one ** STEP)
    second_hat = second_new / (1.0 - beta_two ** STEP)
    master = weights.astype(jnp.float32)
    updated = master - learn_rate * (first_hat / (jnp.sqrt(second_hat) + adam_eps) + decay_rate * master)
    return (updated.astype(jnp.bfloat16), first_new.astype(jnp.bfloat16), second_new.astype(jnp.bfloat16))

def reference(tokens, routing, grad_up, up_shard, error_feedback, moment_one, moment_two, loss_scale):
    block_total = N_EXPERT * N_DP
    capacity = CAP
    expert_total = EXPERTS
    chosen, within, counts = jax.vmap(lambda routes_block: place_pairs(routes_block, expert_total))(routing.reshape(block_total, TOK_DEV * TOP))
    block_ids = jnp.arange(block_total, dtype=jnp.int32)[:, None]
    token_ids = (block_ids * TOK_DEV + jnp.arange(TOK_DEV * TOP, dtype=jnp.int32)[None, :] // TOP).astype(jnp.int32)
    block_grid = jnp.broadcast_to(block_ids, chosen.shape).astype(jnp.int32)
    slot_token = jnp.zeros((expert_total, block_total, capacity), jnp.int32).at[chosen, block_grid, within].set(token_ids)
    slot_live = jnp.arange(capacity, dtype=jnp.int32)[None, None, :] < jnp.transpose(counts)[:, :, None]
    span = expert_total * capacity

    def one_expert(token_grads, expert_id):
        weight = up_shard[expert_id]
        gradient = jnp.zeros((D, FF), jnp.float32)
        for column in range(N_DP):
            picked = slot_token[expert_id][column::N_DP].reshape(-1)
            live_slot = slot_live[expert_id][column::N_DP].reshape(-1)
            gathered = tokens[picked]
            up_rows = grad_up[expert_id, column * span:(column + 1) * span]
            masked = jnp.where(live_slot[:, None], up_rows, jnp.zeros_like(up_rows))
            partial_sum = lax.dot_general(gathered, masked, (((0,), (0,)), ((), ())), preferred_element_type=jnp.float32)
            with_error = partial_sum + error_feedback[expert_id, column * D:(column + 1) * D].astype(jnp.float32)
            levels, block_scale = dequantized(with_error)
            gradient = gradient + (levels.astype(jnp.float32) * block_scale.astype(jnp.float32)[:, :, None]).reshape(D, FF)
            returned = lax.dot_general(masked, weight, (((1,), (1,)), ((), ())), preferred_element_type=jnp.float32).astype(jnp.bfloat16)
            token_grads = token_grads.at[picked].add(jnp.where(live_slot[:, None], returned.astype(jnp.float32), jnp.float32(0.0)))
        gradient = gradient / loss_scale
        new_w, new_m, new_v = adam_update(weight, moment_one[expert_id], moment_two[expert_id], gradient)
        return (token_grads, (new_w, new_m, new_v))
    start_grads = jnp.zeros((TOKENS, D), jnp.float32)
    token_grads, updates = lax.scan(one_expert, start_grads, jnp.arange(expert_total, dtype=jnp.int32))
    return (token_grads.astype(jnp.bfloat16), updates[0], updates[1], updates[2])
```

```python
import jax
import jax.numpy as jnp
from jax import lax
from jax.experimental import pallas as pl
from jax.experimental.pallas import tpu as pltpu
from jax.sharding import Mesh, PartitionSpec as P

D = 2560
FF = 768
TOP = 6
QB = 128
NQ = FF // QB
STEP = 20
TOK = 128
CAP = 36
NX = 4
NZ = 8
NDP = 8
SHARD = D // NDP
INFO = 128
EXT = D + INFO
MSG = SHARD + 16
TILE = 512

learn_rate = 0.001
beta_one = 0.9
beta_two = 0.999
decay_rate = 0.1
adam_eps = 1e-08
quant_top = 127.0
amax_eps = 1e-06

CHUNKS = ((0, -1, 1), (-2, 2), (-3, 3, 4))
ROWS = tuple(-(-len(c) * CAP // 16) * 16 for c in CHUNKS)
bf16 = jnp.bfloat16
f32 = jnp.float32


def params(n=1):
    return pltpu.CompilerParams(dimension_semantics=("arbitrary",) * n)


def prep_kernel(routing_ref, tokens_ref, ext_ref):
    r = routing_ref[...]
    lane = lax.broadcasted_iota(jnp.int32, (TOK, INFO), 1)
    row = lax.broadcasted_iota(jnp.int32, (TOK, INFO), 0)
    named = jnp.zeros((TOK, INFO), f32)
    for k in range(TOP):
        named = named + jnp.where(r[:, k : k + 1] == lane, 1.0, 0.0)
    earlier = jnp.where(row > lane, 1.0, 0.0).astype(bf16)
    before = jnp.dot(earlier, named.astype(bf16), preferred_element_type=f32)
    info = jnp.zeros((TOK, INFO), f32)
    for k in range(TOP):
        e = r[:, k : k + 1]
        w = jnp.sum(jnp.where(e == lane, before, 0.0), axis=1, keepdims=True)
        info = info + jnp.where(lane == k, e.astype(f32), 0.0)
        info = info + jnp.where(lane == TOP + k, w, 0.0)
    ext_ref[:, :D] = tokens_ref[...]
    ext_ref[:, D:] = info.astype(bf16)


def prep(routing, tokens):
    return pl.pallas_call(
        prep_kernel,
        out_shape=jax.ShapeDtypeStruct((TOK, EXT), bf16),
        name="prep",
    )(routing, tokens)


def joined(refs):
    parts = [ref[...] for ref in refs]
    return parts[0] if len(parts) == 1 else jnp.concatenate(parts, axis=0)


def slot_of(e, w, x, z):
    ex = jnp.floor(e * 0.125)
    ez = e - ex * 8.0
    dx = ex - x
    dx = jnp.where(dx < 0.0, dx + float(NX), dx)
    return jnp.where(ez == z, dx * 64.0 + w, -1.0)


def dispatch(me, blocks, rows):
    nb = len(blocks)
    flat = [a for b in blocks for a in b]
    sizes = [len(b) for b in blocks]
    nf = len(flat)

    def kernel(me_ref, *refs):
        tok, inf, outs, hot = refs[:nf], refs[nf : 2 * nf], refs[2 * nf : 2 * nf + NX], refs[-1]

        @pl.when(pl.program_id(0) == 0)
        def _():
            x = me_ref[0].astype(f32)
            z = me_ref[1].astype(f32)
            row = lax.broadcasted_iota(jnp.int32, (rows, TOK), 0).astype(f32)
            at = 0
            for b in range(nb):
                info = jnp.transpose(joined(inf[at : at + sizes[b]]).astype(f32))
                at += sizes[b]
                code = slot_of(info[0:TOP], info[TOP : 2 * TOP], x, z)
                for dx in range(NX):
                    want = jnp.where(
                        (row >= float(CAP * b)) & (row < float(CAP * (b + 1))),
                        row - float(CAP * b) + 64.0 * dx,
                        -2.0,
                    )
                    hit = jnp.zeros((rows, TOK), f32)
                    for k in range(TOP):
                        hit = jnp.where(want == code[k : k + 1, :], 1.0, hit)
                    hot[dx, :, b * TOK : (b + 1) * TOK] = hit.astype(bf16)

        at = 0
        values = []
        for b in range(nb):
            values.append(joined(tok[at : at + sizes[b]]))
            at += sizes[b]
        t = values[0] if nb == 1 else jnp.concatenate(values, axis=0)
        for dx in range(NX):
            outs[dx][...] = jnp.dot(hot[dx], t, preferred_element_type=f32).astype(bf16)

    specs = [pl.BlockSpec((a.shape[0], TILE), lambda i, m: (0, i)) for a in flat]
    specs += [pl.BlockSpec((a.shape[0], INFO), lambda i, m: (0, D // INFO)) for a in flat]
    return pl.pallas_call(
        kernel,
        out_shape=[jax.ShapeDtypeStruct((rows, D), bf16)] * NX,
        grid_spec=pltpu.PrefetchScalarGridSpec(
            num_scalar_prefetch=1,
            grid=(D // TILE,),
            in_specs=specs,
            out_specs=[pl.BlockSpec((rows, TILE), lambda i, m: (0, i))] * NX,
            scratch_shapes=[pltpu.VMEM((NX, rows, nb * TOK), bf16)],
        ),
        compiler_params=params(),
        name="dispatch",
    )(me, *flat, *flat)


def combine(me, rows_in, parts, slots, adds):
    rows = rows_in[0].shape[0]
    nb = len(parts)
    flat = [a for p in parts for a in p]
    sizes = [len(p) for p in parts]
    nf = len(flat)
    added = [a for p in adds for a, _ in p]
    na = len(added)

    def kernel(me_ref, *refs):
        src, inf = refs[:NX], refs[NX : NX + nf]
        extra = refs[NX + nf : NX + nf + na]
        outs = refs[NX + nf + na : NX + nf + na + nb]
        hot = refs[-1]

        @pl.when(pl.program_id(0) == 0)
        def _():
            x = me_ref[0].astype(f32)
            z = me_ref[1].astype(f32)
            lane = lax.broadcasted_iota(jnp.int32, (TOK, rows), 1).astype(f32)
            at = 0
            for b in range(nb):
                info = joined(inf[at : at + sizes[b]]).astype(f32)
                at += sizes[b]
                code = slot_of(info[:, 0:TOP], info[:, TOP : 2 * TOP], x, z)
                first = CAP * slots[b]
                for dx in range(NX):
                    want = jnp.where(
                        (lane >= float(first)) & (lane < float(first + CAP)),
                        lane - float(first) + 64.0 * dx,
                        -2.0,
                    )
                    hit = jnp.zeros((TOK, rows), f32)
                    for k in range(TOP):
                        hit = jnp.where(want == code[:, k : k + 1], 1.0, hit)
                    hot[dx, b * TOK : (b + 1) * TOK, :] = hit.astype(bf16)

        total = jnp.dot(hot[0], src[0][...], preferred_element_type=f32)
        for dx in range(1, NX):
            total = total + jnp.dot(hot[dx], src[dx][...], preferred_element_type=f32)
        at = 0
        for b in range(nb):
            mine = total[b * TOK : (b + 1) * TOK]
            for _, (first, count) in adds[b]:
                more = extra[at][...].astype(f32)
                at += 1
                if count < TOK:
                    pad = jnp.zeros((TOK - count, TILE), f32)
                    more = jnp.concatenate([more, pad] if first == 0 else [pad, more], axis=0)
                mine = mine + more
            outs[b][...] = mine.astype(bf16)

    specs = [pl.BlockSpec((rows, TILE), lambda i, m: (0, i))] * NX
    specs += [pl.BlockSpec((a.shape[0], INFO), lambda i, m: (0, D // INFO)) for a in flat]
    specs += [pl.BlockSpec((a.shape[0], TILE), lambda i, m: (0, i)) for a in added]
    return pl.pallas_call(
        kernel,
        out_shape=[jax.ShapeDtypeStruct((TOK, D), bf16)] * nb,
        grid_spec=pltpu.PrefetchScalarGridSpec(
            num_scalar_prefetch=1,
            grid=(D // TILE,),
            in_specs=specs,
            out_specs=[pl.BlockSpec((TOK, TILE), lambda i, m: (0, i))] * nb,
            scratch_shapes=[pltpu.VMEM((NX, nb * TOK, rows), bf16)],
        ),
        compiler_params=params(),
        name="combine",
    )(me, *rows_in, *flat, *added)


def order_kernel(me_ref, up_ref, *outs):
    x, z = me_ref[0], me_ref[1]
    for c, offsets in enumerate(CHUNKS):
        rows = ROWS[c]
        row = lax.broadcasted_iota(jnp.int32, (rows, NZ * CAP), 0)
        col = lax.broadcasted_iota(jnp.int32, (rows, NZ * CAP), 1)
        want = jnp.full((rows, NZ * CAP), -1, jnp.int32)
        for b, offset in enumerate(offsets):
            block = lax.rem(z + offset + NZ, NZ)
            inside = (row >= CAP * b) & (row < CAP * (b + 1))
            want = jnp.where(inside, block * CAP + row - CAP * b, want)
        pick = jnp.where(want == col, 1.0, 0.0).astype(bf16)
        for dx in range(NX):
            source = lax.rem(x - dx + NX, NX)
            start = pl.multiple_of(source * (NZ * CAP), 16)
            part = up_ref[pl.ds(start, NZ * CAP), :]
            outs[c][dx * rows : (dx + 1) * rows, :] = jnp.dot(
                pick, part, preferred_element_type=f32
            ).astype(bf16)


def ordered(me, up):
    return pl.pallas_call(
        order_kernel,
        out_shape=[jax.ShapeDtypeStruct((NX * r, FF), bf16) for r in ROWS],
        in_specs=[
            pl.BlockSpec(memory_space=pltpu.SMEM),
            pl.BlockSpec(memory_space=pltpu.VMEM),
        ],
        out_specs=[pl.BlockSpec(memory_space=pltpu.VMEM)] * len(ROWS),
        name="order",
    )(me, up)


def slot_grads(ups, weights):
    nc = len(ups)

    def kernel(*refs):
        up, w, outs = refs[:nc], refs[nc], refs[nc + 1 :]
        for c in range(nc):
            for dx in range(NX):
                r = ROWS[c]
                outs[c * NX + dx][...] = lax.dot_general(
                    up[c][dx * r : (dx + 1) * r, :],
                    w[...],
                    (((1,), (1,)), ((), ())),
                    preferred_element_type=f32,
                ).astype(bf16)

    flat_rows = [r for r in ROWS for _ in range(NX)]
    out = pl.pallas_call(
        kernel,
        out_shape=[jax.ShapeDtypeStruct((r, D), bf16) for r in flat_rows],
        grid=(D // TILE,),
        in_specs=[pl.BlockSpec((NX * r, FF), lambda i: (0, 0)) for r in ROWS]
        + [pl.BlockSpec((TILE, FF), lambda i: (i, 0))],
        out_specs=[pl.BlockSpec((r, TILE), lambda i: (0, i)) for r in flat_rows],
        compiler_params=params(),
        name="slot_grads",
    )(*ups, weights)
    return [out[c * NX : (c + 1) * NX] for c in range(nc)]


def levels_of(rows_in, ups, error):
    flat = [a for c in rows_in for a in c]
    nc = len(rows_in)
    wide = 2 * SHARD

    def kernel(*refs):
        src, up, err, out = refs[: len(flat)], refs[len(flat) : len(flat) + nc], refs[-2], refs[-1]
        total = err[...].astype(f32)
        for c in range(nc):
            slab = jnp.concatenate([src[c * NX + dx][...] for dx in range(NX)], axis=0)
            total = total + lax.dot_general(
                slab, up[c][...], (((0,), (0,)), ((), ())), preferred_element_type=f32
            )
        lane = lax.broadcasted_iota(jnp.int32, (wide, QB), 1)
        scales = jnp.zeros((wide, QB), f32)
        for q in range(NQ):
            block = total[:, q * QB : (q + 1) * QB]
            top = jnp.max(jnp.abs(block), axis=1, keepdims=True)
            scale = ((top + amax_eps) / quant_top).astype(bf16).astype(f32)
            level = (block * (1.0 / scale)).astype(bf16)
            out[0, :SHARD, q * QB : (q + 1) * QB] = level[:SHARD]
            out[1, :SHARD, q * QB : (q + 1) * QB] = level[SHARD:]
            scales = jnp.where(lane == q, scale, scales)
        for h in range(2):
            flipped = jnp.transpose(scales[h * SHARD : (h + 1) * SHARD])[:16]
            pad = jnp.zeros((16, FF - SHARD), f32)
            out[h, SHARD:, :] = jnp.concatenate([flipped, pad], axis=1).astype(bf16)

    return pl.pallas_call(
        kernel,
        out_shape=jax.ShapeDtypeStruct((NDP, MSG, FF), bf16),
        grid=(D // wide,),
        in_specs=[pl.BlockSpec((a.shape[0], wide), lambda i: (0, i)) for a in flat]
        + [pl.BlockSpec((NX * r, FF), lambda i: (0, 0)) for r in ROWS]
        + [pl.BlockSpec((wide, FF), lambda i: (i, 0))],
        out_specs=pl.BlockSpec((2, MSG, FF), lambda i: (i, 0, 0)),
        compiler_params=params(),
        name="levels",
    )(*flat, *ups, error)


def adam_kernel(loss_ref, got_ref, scale_ref, w_ref, m_ref, v_ref, nw_ref, nm_ref, nv_ref, sc_ref):
    q = pl.program_id(0)

    @pl.when(q == 0)
    def _():
        for d in range(NDP):
            sc_ref[:, d, :] = scale_ref[d].astype(f32)[:, :384]

    scales = jnp.transpose(sc_ref[q])
    total = jnp.zeros((SHARD, QB), f32)
    for d in range(NDP):
        total = total + got_ref[d].astype(f32) * scales[:SHARD, d : d + 1]
    gradient = total / loss_ref[0]
    first = beta_one * m_ref[...].astype(f32) + (1.0 - beta_one) * gradient
    second = beta_two * v_ref[...].astype(f32) + (1.0 - beta_two) * gradient * gradient
    first_hat = first / (1.0 - beta_one**STEP)
    second_hat = second / (1.0 - beta_two**STEP)
    master = w_ref[...].astype(f32)
    updated = master - learn_rate * (
        first_hat / (jnp.sqrt(second_hat) + adam_eps) + decay_rate * master
    )
    nw_ref[...] = updated.astype(bf16)
    nm_ref[...] = first.astype(bf16)
    nv_ref[...] = second.astype(bf16)


def adam(loss, got, w, m, v):
    column = pl.BlockSpec((SHARD, QB), lambda i: (0, i))
    return pl.pallas_call(
        adam_kernel,
        out_shape=[jax.ShapeDtypeStruct((SHARD, FF), bf16)] * 3,
        grid=(NQ,),
        in_specs=[
            pl.BlockSpec(memory_space=pltpu.SMEM),
            pl.BlockSpec((NDP, SHARD, QB), lambda i: (0, 0, i)),
            pl.BlockSpec((NDP, 16, FF), lambda i: (0, SHARD // 16, 0)),
            column,
            column,
            column,
        ],
        out_specs=[column] * 3,
        scratch_shapes=[pltpu.VMEM((16, NDP, 384), f32)],
        compiler_params=params(),
        name="adam",
    )(loss, got, got, w, m, v)


def on_device(tokens, routing, grad_up, up_shard, error_feedback, moment_one, moment_two, loss):
    def along(axis, n, shift):
        return lambda a: lax.ppermute(a, axis, [(i, (i + shift) % n) for i in range(n)])

    up_z, down_z = along("z", NZ, 1), along("z", NZ, -1)
    me = jnp.stack([lax.axis_index("x"), lax.axis_index("z")]).astype(jnp.int32)
    weights = lax.all_gather(up_shard[0], "dp", axis=0, tiled=True)

    ext = prep(routing, tokens)
    block = {0: [ext]}
    up, down = ext, ext
    for r in (1, 2, 3):
        up, down = up_z(up), down_z(down)
        block[-r], block[r] = [up], [down]
    block[4] = [up_z(up[: TOK // 2]), down_z(down[TOK // 2 :])]

    arrived = []
    for offsets, rows in zip(CHUNKS, ROWS):
        out = dispatch(me, [block[o] for o in offsets], rows)
        arrived.append([out[0]] + [along("x", NX, dx)(out[dx]) for dx in range(1, NX)])

    ups = ordered(me, grad_up[0])
    packed = levels_of(arrived, ups, error_feedback[0])
    got = lax.all_to_all(packed, "dp", split_axis=0, concat_axis=0, tiled=True)
    new_w, new_m, new_v = adam(
        loss.reshape(1), got, up_shard[0], moment_one[0], moment_two[0]
    )
    full = lax.all_gather(new_w, "dp", axis=0, tiled=True)

    returned = slot_grads(ups, weights)
    back = [None] * len(CHUNKS)
    for c in reversed(range(len(CHUNKS))):
        out = returned[c]
        back[c] = [out[0]] + [along("x", NX, -dx)(out[dx]) for dx in range(1, NX)]
    half = TOK // 2
    (far,) = combine(me, back[2], [block[4]], [2], [[]])
    fwd, bwd = up_z(far[:half]), down_z(far[half:])
    top, low = (0, half), (half, half)
    whole = (0, TOK)
    q_up, q_down = combine(
        me, back[2], [block[3], block[-3]], [1, 0], [[(fwd, top)], [(bwd, low)]]
    )
    q_up, q_down = up_z(q_up), down_z(q_down)
    q_up, q_down = combine(
        me, back[1], [block[2], block[-2]], [1, 0], [[(q_up, whole)], [(q_down, whole)]]
    )
    q_up, q_down = up_z(q_up), down_z(q_down)
    q_up, q_down = combine(
        me, back[0], [block[1], block[-1]], [2, 1], [[(q_up, whole)], [(q_down, whole)]]
    )
    q_up, q_down = up_z(q_up), down_z(q_down)
    (grad_tokens,) = combine(
        me, back[0], [block[0]], [0], [[(q_up, whole), (q_down, whole)]]
    )
    return (grad_tokens, full[None], new_m[None], new_v[None])


def solution(mesh):
    fine = Mesh(mesh.devices.reshape(NX, NZ, NDP), ("x", "z", "dp"))
    expert = ("x", "z")
    in_specs = (
        P(("x", "z", "dp"), None),
        P(("x", "z", "dp"), None),
        P(expert, "dp", None),
        P(expert, "dp", None),
        P(expert, "dp", None),
        P(expert, "dp", None),
        P(expert, "dp", None),
        P(),
    )
    out_specs = (
        P(("x", "z", "dp"), None),
        P(expert, None, None),
        P(expert, "dp", None),
        P(expert, "dp", None),
    )
    return jax.shard_map(
        on_device, mesh=fine, in_specs=in_specs, out_specs=out_specs, check_vma=False
    )
```

```python
import jax
import jax.numpy as jnp
from jax import lax
from jax.experimental import pallas as pl
from jax.experimental.pallas import tpu as pltpu
from jax.sharding import Mesh, PartitionSpec as P

D = 2560
FF = 768
TOP = 6
QB = 128
NQ = FF // QB
STEP = 20
TOK = 128
CAP = 36
NX = 4
NZ = 8
NDP = 8
SHARD = D // NDP
INFO = 128
EXT = D + INFO
MSG = SHARD + 16
TILE = 512

learn_rate = 0.001
beta_one = 0.9
beta_two = 0.999
decay_rate = 0.1
adam_eps = 1e-08
quant_top = 127.0
amax_eps = 1e-06

CHUNKS = ((0, -1, 1), (-2, 2), (-3, 3, 4))
ROWS = tuple(-(-len(c) * CAP // 16) * 16 for c in CHUNKS)
bf16 = jnp.bfloat16
f32 = jnp.float32


VMEM = pltpu.MemorySpace.VMEM
SMEM_SPEC = pl.BlockSpec(memory_space=pltpu.MemorySpace.SMEM)
VMEM_SPEC = pl.BlockSpec(memory_space=VMEM)
STARTS = tuple(NX * sum(ROWS[:c]) for c in range(len(ROWS)))
ALL_ROWS = NX * sum(ROWS)


def params(n=0, mib=6):
    if n == 0:
        return pltpu.CompilerParams(vmem_limit_bytes=mib << 20)
    return pltpu.CompilerParams(
        dimension_semantics=("arbitrary",) * n, vmem_limit_bytes=mib << 20
    )


def near(arrays):
    return [pltpu.with_memory_space_constraint(a, VMEM) for a in arrays]


def prep_kernel(routing_ref, tokens_ref, ext_ref):
    r = routing_ref[...]
    down = lax.broadcasted_iota(jnp.int32, (INFO, TOK), 0)
    across = lax.broadcasted_iota(jnp.int32, (INFO, TOK), 1)
    named = jnp.zeros((INFO, TOK), f32)
    for k in range(TOP):
        named = named + jnp.where(r[k : k + 1, :] == down, 1.0, 0.0)
    earlier = jnp.where(down < across, 1.0, 0.0).astype(bf16)
    before = jnp.dot(named.astype(bf16), earlier, preferred_element_type=f32)
    info = jnp.zeros((INFO, TOK), f32)
    for k in range(TOP):
        e = r[k : k + 1, :]
        w = jnp.sum(jnp.where(e == down, before, 0.0), axis=0, keepdims=True)
        info = jnp.where(down == k, e.astype(f32), info)
        info = jnp.where(down == TOP + k, w, info)
    ext_ref[:, :D] = tokens_ref[...]
    ext_ref[:, D:] = jnp.transpose(info).astype(bf16)


def prep(routing, tokens):
    return pl.pallas_call(
        prep_kernel,
        out_shape=pltpu.VMEM((TOK, EXT), bf16),
        in_specs=[VMEM_SPEC] * 2,
        out_specs=VMEM_SPEC,
        compiler_params=params(),
        name="prep",
    )(routing, tokens)


def joined(parts):
    return parts[0] if len(parts) == 1 else jnp.concatenate(parts, axis=0)


def slot_of(e, w, x, z):
    ex = jnp.floor(e * 0.125)
    ez = e - ex * 8.0
    dx = ex - x
    dx = jnp.where(dx < 0.0, dx + float(NX), dx)
    return jnp.where(ez == z, dx * 64.0 + w, -1.0)


def dispatch(me, blocks, rows):
    nb = len(blocks)
    flat = [a for b in blocks for a in b]
    sizes = [len(b) for b in blocks]
    nf = len(flat)

    def kernel(me_ref, *refs):
        tok, outs, codes, hot = refs[:nf], refs[nf : nf + NX], refs[nf + NX], refs[-1]
        x = me_ref[0].astype(f32)
        z = me_ref[1].astype(f32)
        row = lax.broadcasted_iota(jnp.int32, (rows, TOK), 0).astype(f32)
        at = 0
        for b in range(nb):
            raw = joined([t[:, D:] for t in tok[at : at + sizes[b]]]).astype(f32)
            at += sizes[b]
            codes[b * TOK : (b + 1) * TOK, :] = slot_of(
                raw, pltpu.roll(raw, INFO - TOP, 1), x, z
            ).astype(bf16)
            info = jnp.transpose(raw)
            code = slot_of(info[0:TOP], info[TOP : 2 * TOP], x, z)
            for dx in range(NX):
                want = jnp.where(
                    (row >= float(CAP * b)) & (row < float(CAP * (b + 1))),
                    row - float(CAP * b) + 64.0 * dx,
                    -2.0,
                )
                hit = jnp.zeros((rows, TOK), f32)
                for k in range(TOP):
                    hit = jnp.where(want == code[k : k + 1, :], 1.0, hit)
                hot[dx * rows : (dx + 1) * rows, b * TOK : (b + 1) * TOK] = hit.astype(bf16)

        def column(i, _):
            where = pl.ds(pl.multiple_of(i * TILE, TILE), TILE)
            t = joined([t[:, where] for t in tok])
            got = jnp.dot(hot[...], t, preferred_element_type=f32).astype(bf16)
            for dx in range(NX):
                outs[dx][:, where] = got[dx * rows : (dx + 1) * rows]
            return 0

        lax.fori_loop(0, D // TILE, column, 0)

    out = pl.pallas_call(
        kernel,
        out_shape=[pltpu.VMEM((rows, D), bf16)] * NX
        + [jax.ShapeDtypeStruct((nb * TOK, INFO), bf16)],
        in_specs=[SMEM_SPEC] + [VMEM_SPEC] * nf,
        out_specs=[VMEM_SPEC] * (NX + 1),
        scratch_shapes=[pltpu.VMEM((NX * rows, nb * TOK), bf16)],
        compiler_params=params(),
        name="dispatch",
    )(me, *near(flat))
    return out[:NX], out[NX]


def hots_kernel(*refs):
    nc = len(CHUNKS)
    for c, offsets in enumerate(CHUNKS):
        codes, out, rows = refs[c], refs[nc + c], ROWS[c]
        lane = lax.broadcasted_iota(jnp.int32, (TOK, rows), 1).astype(f32)
        for b in range(len(offsets)):
            code = codes[b * TOK : (b + 1) * TOK, :].astype(f32)
            first = CAP * b
            for dx in range(NX):
                want = jnp.where(
                    (lane >= float(first)) & (lane < float(first + CAP)),
                    lane - float(first) + 64.0 * dx,
                    -2.0,
                )
                hit = jnp.zeros((TOK, rows), f32)
                for k in range(TOP):
                    hit = jnp.where(want == code[:, k : k + 1], 1.0, hit)
                out[b * TOK : (b + 1) * TOK, dx * rows : (dx + 1) * rows] = hit.astype(bf16)


def hots(codes):
    return pl.pallas_call(
        hots_kernel,
        out_shape=[
            pltpu.VMEM((len(o) * TOK, NX * r), bf16) for o, r in zip(CHUNKS, ROWS)
        ],
        in_specs=[VMEM_SPEC] * len(CHUNKS),
        out_specs=[VMEM_SPEC] * len(CHUNKS),
        compiler_params=params(),
        name="hots",
    )(*codes)


def combine(hot, rows_in, slots, adds, last=False, split=1):
    nb = len(slots)
    added = [a for p in adds for a, _ in p]
    na = len(added)

    def kernel(hot_ref, *refs):
        src, extra, outs = refs[:NX], refs[NX : NX + na], refs[NX + na :]

        def column(i, _):
            where = pl.ds(pl.multiple_of(i * TILE, TILE), TILE)
            data = jnp.concatenate([s[:, where] for s in src], axis=0)
            at = 0
            for b in range(nb):
                mine = jnp.dot(
                    hot_ref[slots[b] * TOK : (slots[b] + 1) * TOK, :],
                    data,
                    preferred_element_type=f32,
                )
                for _, (first, count) in adds[b]:
                    more = extra[at][:, where].astype(f32)
                    at += 1
                    if count < TOK:
                        pad = jnp.zeros((TOK - count, TILE), f32)
                        more = jnp.concatenate(
                            [more, pad] if first == 0 else [pad, more], axis=0
                        )
                    mine = mine + more
                mine = mine.astype(bf16)
                part = TOK // split
                for h in range(split):
                    outs[b * split + h][:, where] = mine[h * part : (h + 1) * part]
            return 0

        lax.fori_loop(0, D // TILE, column, 0)

    kind = (lambda s, t: jax.ShapeDtypeStruct(s, t)) if last else pltpu.VMEM
    return pl.pallas_call(
        kernel,
        out_shape=[kind((TOK // split, D), bf16)] * (nb * split),
        in_specs=[VMEM_SPEC] * (1 + NX + na),
        out_specs=[VMEM_SPEC] * (nb * split),
        compiler_params=params(),
        name="combine",
    )(*near([hot, *rows_in, *added]))


def order_kernel(me_ref, up_ref, out):
    x, z = me_ref[0], me_ref[1]
    for c, offsets in enumerate(CHUNKS):
        rows = ROWS[c]
        row = lax.broadcasted_iota(jnp.int32, (rows, NZ * CAP), 0)
        col = lax.broadcasted_iota(jnp.int32, (rows, NZ * CAP), 1)
        want = jnp.full((rows, NZ * CAP), -1, jnp.int32)
        for b, offset in enumerate(offsets):
            block = lax.rem(z + offset + NZ, NZ)
            inside = (row >= CAP * b) & (row < CAP * (b + 1))
            want = jnp.where(inside, block * CAP + row - CAP * b, want)
        pick = jnp.where(want == col, 1.0, 0.0).astype(bf16)
        for dx in range(NX):
            source = lax.rem(x - dx + NX, NX)
            start = pl.multiple_of(source * (NZ * CAP), 16)
            part = up_ref[pl.ds(start, NZ * CAP), :]
            at = STARTS[c] + dx * rows
            out[at : at + rows, :] = jnp.dot(pick, part, preferred_element_type=f32).astype(bf16)


def ordered(me, up):
    return pl.pallas_call(
        order_kernel,
        out_shape=jax.ShapeDtypeStruct((ALL_ROWS, FF), bf16),
        in_specs=[SMEM_SPEC, VMEM_SPEC],
        out_specs=VMEM_SPEC,
        compiler_params=params(),
        name="order",
    )(me, up)


def slot_grads(ups, weights):
    flat_rows = [r for r in ROWS for _ in range(NX)]

    def kernel(up, w, *outs):
        got = lax.dot_general(
            up[...], w[...], (((1,), (1,)), ((), ())), preferred_element_type=f32
        ).astype(bf16)
        at = 0
        for out, r in zip(outs, flat_rows):
            out[...] = got[at : at + r]
            at += r

    out = pl.pallas_call(
        kernel,
        out_shape=[pltpu.HBM((r, D), bf16) for r in flat_rows],
        grid=(D // TILE,),
        in_specs=[
            pl.BlockSpec((ALL_ROWS, FF), lambda i: (0, 0)),
            pl.BlockSpec((TILE, FF), lambda i: (i, 0)),
        ],
        out_specs=[pl.BlockSpec((r, TILE), lambda i: (0, i)) for r in flat_rows],
        compiler_params=params(1, 16),
        name="slot_grads",
    )(ups, weights)
    return [out[c * NX : (c + 1) * NX] for c in range(len(ROWS))]


def levels_of(rows_in, ups, error):
    flat = [a for c in rows_in for a in c]
    wide = 2 * SHARD

    def kernel(*refs):
        src, up, err, out = refs[: len(flat)], refs[-3], refs[-2], refs[-1]
        slab = jnp.concatenate([s[...] for s in src], axis=0)
        total = err[...].astype(f32) + lax.dot_general(
            slab, up[...], (((0,), (0,)), ((), ())), preferred_element_type=f32
        )
        lane = lax.broadcasted_iota(jnp.int32, (wide, QB), 1)
        scales = jnp.zeros((wide, QB), f32)
        for q in range(NQ):
            block = total[:, q * QB : (q + 1) * QB]
            top = jnp.max(jnp.abs(block), axis=1, keepdims=True)
            scale = ((top + amax_eps) / quant_top).astype(bf16).astype(f32)
            level = (block * (1.0 / scale)).astype(bf16)
            out[0, :SHARD, q * QB : (q + 1) * QB] = level[:SHARD]
            out[1, :SHARD, q * QB : (q + 1) * QB] = level[SHARD:]
            scales = jnp.where(lane == q, scale, scales)
        for h in range(2):
            flipped = jnp.transpose(scales[h * SHARD : (h + 1) * SHARD])[:16]
            pad = jnp.zeros((16, FF - SHARD), f32)
            out[h, SHARD:, :] = jnp.concatenate([flipped, pad], axis=1).astype(bf16)

    return pl.pallas_call(
        kernel,
        out_shape=pltpu.HBM((NDP, MSG, FF), bf16),
        grid=(D // wide,),
        in_specs=[pl.BlockSpec((a.shape[0], wide), lambda i: (0, i)) for a in flat]
        + [pl.BlockSpec((ALL_ROWS, FF), lambda i: (0, 0))]
        + [pl.BlockSpec((wide, FF), lambda i: (i, 0))],
        out_specs=pl.BlockSpec((2, MSG, FF), lambda i: (i, 0, 0)),
        compiler_params=params(1, 24),
        name="levels",
    )(*flat, ups, error)


def adam_kernel(loss_ref, got_ref, scale_ref, w_ref, m_ref, v_ref, nw_ref, nm_ref, nv_ref, sc_ref):
    q = pl.program_id(0)

    @pl.when(q == 0)
    def _():
        for d in range(NDP):
            sc_ref[:, d, :] = scale_ref[d].astype(f32)[:, :384]

    scales = jnp.transpose(sc_ref[q])
    total = jnp.zeros((SHARD, QB), f32)
    for d in range(NDP):
        total = total + got_ref[d].astype(f32) * scales[:SHARD, d : d + 1]
    gradient = total / loss_ref[0]
    first = beta_one * m_ref[...].astype(f32) + (1.0 - beta_one) * gradient
    second = beta_two * v_ref[...].astype(f32) + (1.0 - beta_two) * gradient * gradient
    first_hat = first / (1.0 - beta_one**STEP)
    second_hat = second / (1.0 - beta_two**STEP)
    master = w_ref[...].astype(f32)
    updated = master - learn_rate * (
        first_hat / (jnp.sqrt(second_hat) + adam_eps) + decay_rate * master
    )
    nw_ref[0] = updated.astype(bf16)
    nm_ref[...] = first.astype(bf16)
    nv_ref[...] = second.astype(bf16)


def adam(loss, got, w, m, v):
    column = pl.BlockSpec((SHARD, QB), lambda i: (0, i))
    return pl.pallas_call(
        adam_kernel,
        out_shape=[pltpu.HBM((1, SHARD, FF), bf16)]
        + [pltpu.HBM((SHARD, FF), bf16)] * 2,
        grid=(NQ,),
        in_specs=[
            pl.BlockSpec(memory_space=pltpu.SMEM),
            pl.BlockSpec((NDP, SHARD, QB), lambda i: (0, 0, i)),
            pl.BlockSpec((NDP, 16, FF), lambda i: (0, SHARD // 16, 0)),
            column,
            column,
            column,
        ],
        out_specs=[pl.BlockSpec((1, SHARD, QB), lambda i: (0, 0, i)), column, column],
        scratch_shapes=[pltpu.VMEM((16, NDP, 384), f32)],
        compiler_params=params(1, 8),
        name="adam",
    )(loss, got, got, w, m, v)


def step(tokens, routing, grad_up, up_shard, error_feedback, moment_one, moment_two, loss):
    def send(a, axis, n, shift):
        pairs = [(i, (i + shift) % n) for i in range(n)]
        return lax.ppermute(a, axis, pairs)

    def send_x(arrays, sign):
        return [arrays[0]] + [send(arrays[dx], "x", NX, sign * dx) for dx in range(1, NX)]

    def send_z(a, b):
        return send(a, "z", NZ, 1), send(b, "z", NZ, -1)

    me = jnp.stack([lax.axis_index("x"), lax.axis_index("z")]).astype(jnp.int32)
    weights = lax.all_gather(up_shard[0], "dp", axis=0, tiled=True)

    half = TOK // 2
    ext = prep(jnp.transpose(routing), tokens)
    block = {0: [ext]}
    up, down = ext, ext
    for r in (1, 2, 3):
        up, down = send_z(up, down)
        block[-r], block[r] = [up], [down]
    block[4] = list(send_z(up[:half], down[half:]))

    arrived, codes = [], []
    for offsets, rows in zip(CHUNKS, ROWS):
        out, code = dispatch(me, [block[o] for o in offsets], rows)
        arrived.append(send_x(out, 1))
        codes.append(code)
    hot = hots(codes)

    ups = ordered(me, grad_up[0])
    returned = slot_grads(ups, weights)
    packed = levels_of(arrived, ups, error_feedback[0])
    got = lax.all_to_all(packed, "dp", split_axis=0, concat_axis=0, tiled=True)
    new_w, new_m, new_v = adam(loss.reshape(1), got, up_shard[0], moment_one[0], moment_two[0])
    full = lax.all_gather(new_w, "dp", axis=1, tiled=True)

    back = [None] * len(CHUNKS)
    for c in reversed(range(len(CHUNKS))):
        back[c] = send_x(returned[c], -1)
    top, low, whole = (0, half), (half, half), (0, TOK)
    u, d = combine(hot[2], back[2], [2], [[]], split=2)
    u, d = send_z(u, d)
    u, d = combine(hot[2], back[2], [1, 0], [[(u, top)], [(d, low)]])
    u, d = send_z(u, d)
    u, d = combine(hot[1], back[1], [1, 0], [[(u, whole)], [(d, whole)]])
    u, d = send_z(u, d)
    u, d = combine(hot[0], back[0], [2, 1], [[(u, whole)], [(d, whole)]])
    u, d = send_z(u, d)
    (grad_tokens,) = combine(hot[0], back[0], [0], [[(u, whole), (d, whole)]], last=True)
    return (grad_tokens, full, new_m[None], new_v[None])


def solution(mesh):
    fine = Mesh(mesh.devices.reshape(NX, NZ, NDP), ("x", "z", "dp"))
    expert = ("x", "z")
    in_specs = (
        P(("x", "z", "dp"), None),
        P(("x", "z", "dp"), None),
        P(expert, "dp", None),
        P(expert, "dp", None),
        P(expert, "dp", None),
        P(expert, "dp", None),
        P(expert, "dp", None),
        P(),
    )
    out_specs = (
        P(("x", "z", "dp"), None),
        P(expert, None, None),
        P(expert, "dp", None),
        P(expert, "dp", None),
    )
    return jax.shard_map(step, mesh=fine, in_specs=in_specs, out_specs=out_specs, check_vma=False)
```

```python
import jax
import jax.numpy as jnp
from jax import lax
from jax.experimental import pallas as pl
from jax.experimental.pallas import tpu as pltpu
from jax.sharding import Mesh, PartitionSpec as P

D = 2560
FF = 768
TOP = 6
QB = 128
NQ = FF // QB
STEP = 20
TOK = 128
CAP = 36
NX = 4
NZ = 8
NDP = 8
NY = 4
SHARD = D // NDP
INFO = 128
EXT = D + INFO
WIDE = FF + 128
TILE = 512

learn_rate = 0.001
beta_one = 0.9
beta_two = 0.999
decay_rate = 0.1
adam_eps = 1e-08
quant_top = 127.0
amax_eps = 1e-06

CHUNKS = ((0,), (-1, 1), (-2, 2), (-3, 3), (4,))
ROWS = tuple(-(-len(c) * CAP // 8) * 8 for c in CHUNKS)
bf16 = jnp.bfloat16
f32 = jnp.float32


VMEM = pltpu.MemorySpace.VMEM
SMEM_SPEC = pl.BlockSpec(memory_space=pltpu.MemorySpace.SMEM)
VMEM_SPEC = pl.BlockSpec(memory_space=VMEM)
STARTS = tuple(NX * sum(ROWS[:c]) for c in range(len(ROWS)))
ALL_ROWS = NX * sum(ROWS)


def params(n=0, mib=6):
    if n == 0:
        return pltpu.CompilerParams(vmem_limit_bytes=mib << 20)
    return pltpu.CompilerParams(
        dimension_semantics=("arbitrary",) * n, vmem_limit_bytes=mib << 20
    )


def near(arrays):
    return [pltpu.with_memory_space_constraint(a, VMEM) for a in arrays]


def prep_kernel(routing_ref, tokens_ref, ext_ref):
    r = routing_ref[...]
    down = lax.broadcasted_iota(jnp.int32, (INFO, TOK), 0)
    across = lax.broadcasted_iota(jnp.int32, (INFO, TOK), 1)
    named = jnp.zeros((INFO, TOK), f32)
    for k in range(TOP):
        named = named + jnp.where(r[k : k + 1, :] == down, 1.0, 0.0)
    earlier = jnp.where(down < across, 1.0, 0.0).astype(bf16)
    before = jnp.dot(named.astype(bf16), earlier, preferred_element_type=f32)
    info = jnp.zeros((INFO, TOK), f32)
    for k in range(TOP):
        e = r[k : k + 1, :]
        w = jnp.sum(jnp.where(e == down, before, 0.0), axis=0, keepdims=True)
        info = jnp.where(down == k, e.astype(f32), info)
        info = jnp.where(down == TOP + k, w, info)
    ext_ref[:, :D] = tokens_ref[...]
    ext_ref[:, D:] = jnp.transpose(info).astype(bf16)


def prep(routing, tokens):
    return pl.pallas_call(
        prep_kernel,
        out_shape=pltpu.VMEM((TOK, EXT), bf16),
        in_specs=[VMEM_SPEC] * 2,
        out_specs=VMEM_SPEC,
        compiler_params=params(),
        name="prep",
    )(routing, tokens)


def stacked(parts):
    return jnp.concatenate([p.astype(f32) for p in parts], axis=0).astype(bf16)


def joined(parts):
    return parts[0] if len(parts) == 1 else jnp.concatenate(parts, axis=0)


def slot_of(e, w, x, z):
    ex = jnp.floor(e * 0.125)
    ez = e - ex * 8.0
    dx = ex - x
    dx = jnp.where(dx < 0.0, dx + float(NX), dx)
    return jnp.where(ez == z, dx * 64.0 + w, -1.0)


def placed(at, rows):
    side = jnp.floor((at + 0.5) * (1.0 / rows))
    return at - side * float(rows), side


def wanted(row, side, b):
    inside = (row >= float(CAP * b)) & (row < float(CAP * (b + 1)))
    return jnp.where(inside, row - float(CAP * b) + 64.0 * side, -2.0)


def dispatch(me, blocks, rows):
    nb = len(blocks)
    flat = [a for b in blocks for a in b]
    sizes = [len(b) for b in blocks]
    nf = len(flat)

    def kernel(me_ref, *refs):
        tok, outs, codes, hot = refs[:nf], refs[nf : nf + NX], refs[nf + NX], refs[-1]
        x = me_ref[0].astype(f32)
        z = me_ref[1].astype(f32)
        row = lax.broadcasted_iota(jnp.int32, (NX * rows, TOK), 0).astype(f32)
        row, side = placed(row, rows)
        at = 0
        for b in range(nb):
            raw = joined([t[:, D:] for t in tok[at : at + sizes[b]]]).astype(f32)
            at += sizes[b]
            codes[b * TOK : (b + 1) * TOK, :] = slot_of(
                raw, pltpu.roll(raw, INFO - TOP, 1), x, z
            ).astype(bf16)
            info = jnp.transpose(raw)
            code = slot_of(info[0:TOP], info[TOP : 2 * TOP], x, z)
            want = wanted(row, side, b)
            hit = jnp.zeros((NX * rows, TOK), f32)
            for k in range(TOP):
                hit = jnp.where(want == code[k : k + 1, :], 1.0, hit)
            hot[:, b * TOK : (b + 1) * TOK] = hit.astype(bf16)

        def column(i, _):
            where = pl.ds(pl.multiple_of(i * TILE, TILE), TILE)
            t = joined([t[:, where] for t in tok])
            got = jnp.dot(hot[...], t, preferred_element_type=f32)
            for dx in range(NX):
                outs[dx][:, where] = got[dx * rows : (dx + 1) * rows].astype(bf16)
            return 0

        lax.fori_loop(0, D // TILE, column, 0)

    out = pl.pallas_call(
        kernel,
        out_shape=[pltpu.VMEM((rows, D), bf16)] * NX
        + [jax.ShapeDtypeStruct((nb * TOK, INFO), bf16)],
        in_specs=[SMEM_SPEC] + [VMEM_SPEC] * nf,
        out_specs=[VMEM_SPEC] * (NX + 1),
        scratch_shapes=[pltpu.VMEM((NX * rows, nb * TOK), bf16)],
        compiler_params=params(),
        name="dispatch",
    )(me, *near(flat))
    return out[:NX], out[NX]


def hots(codes, chunks):
    nc = len(chunks)

    def kernel(*refs):
        for i, c in enumerate(chunks):
            codes_ref, out, rows = refs[i], refs[nc + i], ROWS[c]
            lane = lax.broadcasted_iota(jnp.int32, (TOK, NX * rows), 1).astype(f32)
            row, side = placed(lane, rows)
            for b in range(len(CHUNKS[c])):
                code = codes_ref[b * TOK : (b + 1) * TOK, :].astype(f32)
                want = wanted(row, side, b)
                hit = jnp.zeros((TOK, NX * rows), f32)
                for k in range(TOP):
                    hit = jnp.where(want == code[:, k : k + 1], 1.0, hit)
                out[b * TOK : (b + 1) * TOK, :] = hit.astype(bf16)

    return pl.pallas_call(
        kernel,
        out_shape=[pltpu.VMEM((len(CHUNKS[c]) * TOK, NX * ROWS[c]), bf16) for c in chunks],
        in_specs=[VMEM_SPEC] * nc,
        out_specs=[VMEM_SPEC] * nc,
        compiler_params=params(),
        name="hots",
    )(*codes)


def combine(hot, rows_in, slots, adds, last=False, split=1):
    nb = len(slots)
    added = [a for p in adds for a, _ in p]
    na = len(added)

    def kernel(hot_ref, *refs):
        src, extra, outs = refs[:NX], refs[NX : NX + na], refs[NX + na :]

        def column(i, _):
            where = pl.ds(pl.multiple_of(i * TILE, TILE), TILE)
            data = stacked([s[:, where] for s in src])
            at = 0
            for b in range(nb):
                mine = jnp.dot(
                    hot_ref[slots[b] * TOK : (slots[b] + 1) * TOK, :],
                    data,
                    preferred_element_type=f32,
                )
                for _, (first, count) in adds[b]:
                    more = extra[at][:, where].astype(f32)
                    at += 1
                    if count < TOK:
                        pad = jnp.zeros((TOK - count, TILE), f32)
                        more = jnp.concatenate(
                            [more, pad] if first == 0 else [pad, more], axis=0
                        )
                    mine = mine + more
                mine = mine.astype(bf16)
                part = TOK // split
                for h in range(split):
                    outs[b * split + h][:, where] = mine[h * part : (h + 1) * part]
            return 0

        lax.fori_loop(0, D // TILE, column, 0)

    kind = (lambda s, t: jax.ShapeDtypeStruct(s, t)) if last else pltpu.VMEM
    return pl.pallas_call(
        kernel,
        out_shape=[kind((TOK // split, D), bf16)] * (nb * split),
        in_specs=[VMEM_SPEC] * (1 + NX + na),
        out_specs=[VMEM_SPEC] * (nb * split),
        compiler_params=params(),
        name="combine",
    )(*near([hot, *rows_in, *added]))


def order_kernel(me_ref, up_ref, out):
    x, z = me_ref[0], me_ref[1]
    for c, offsets in enumerate(CHUNKS):
        rows = ROWS[c]
        row = lax.broadcasted_iota(jnp.int32, (rows, NZ * CAP), 0)
        col = lax.broadcasted_iota(jnp.int32, (rows, NZ * CAP), 1)
        want = jnp.full((rows, NZ * CAP), -1, jnp.int32)
        for b, offset in enumerate(offsets):
            block = lax.rem(z + offset + NZ, NZ)
            inside = (row >= CAP * b) & (row < CAP * (b + 1))
            want = jnp.where(inside, block * CAP + row - CAP * b, want)
        pick = jnp.where(want == col, 1.0, 0.0).astype(bf16)
        got = []
        for dx in range(NX):
            source = lax.rem(x - dx + NX, NX)
            start = pl.multiple_of(source * (NZ * CAP), 16)
            part = up_ref[pl.ds(start, NZ * CAP), :]
            got.append(jnp.dot(pick, part, preferred_element_type=f32))
        out[STARTS[c] : STARTS[c] + NX * rows, :] = jnp.concatenate(got, axis=0).astype(bf16)


def ordered(me, up):
    return pl.pallas_call(
        order_kernel,
        out_shape=jax.ShapeDtypeStruct((ALL_ROWS, FF), bf16),
        in_specs=[SMEM_SPEC, VMEM_SPEC],
        out_specs=VMEM_SPEC,
        compiler_params=params(),
        name="order",
    )(me, up)


def slot_grads(me, ups, same, other):
    flat_rows = [r for r in ROWS for _ in range(NX)]
    wide = 2 * SHARD

    def kernel(me_ref, up, mine, theirs, *outs):
        first = me_ref[3] == 0

        def chip(i, _):
            a, b = mine[i], theirs[i]
            w = jnp.concatenate([jnp.where(first, a, b), jnp.where(first, b, a)], axis=0)
            where = pl.ds(pl.multiple_of(i * wide, 128), wide)
            got = lax.dot_general(
                up[...], w, (((1,), (1,)), ((), ())), preferred_element_type=f32
            )
            at = 0
            for out, r in zip(outs, flat_rows):
                out[:, where] = got[at : at + r].astype(bf16)
                at += r
            return 0

        lax.fori_loop(0, NY, chip, 0)

    out = pl.pallas_call(
        kernel,
        out_shape=[pltpu.VMEM((r, D), bf16) for r in flat_rows],
        in_specs=[SMEM_SPEC] + [VMEM_SPEC] * 3,
        out_specs=[VMEM_SPEC] * len(flat_rows),
        compiler_params=params(mib=12),
        name="slot_grads",
    )(me, *near([ups, same, other]))
    return [out[c * NX : (c + 1) * NX] for c in range(len(ROWS))]


def levels_of(me, rows_in, ups, error):
    flat = [a for c in rows_in for a in c]
    wide = 2 * SHARD

    def kernel(me_ref, *refs):
        src, up, err, keep, give = refs[: len(flat)], refs[-4], refs[-3], refs[-2], refs[-1]
        slab = stacked([s[...] for s in src])
        total = err[...].astype(f32) + lax.dot_general(
            slab, up[...], (((0,), (0,)), ((), ())), preferred_element_type=f32
        )
        first = me_ref[3] == 0
        lane = lax.broadcasted_iota(jnp.int32, (wide, QB), 1)
        scales = jnp.zeros((wide, QB), f32)

        def store(value, columns):
            a, b = value[:SHARD].astype(bf16), value[SHARD:].astype(bf16)
            keep[0, :, columns] = jnp.where(first, a, b)
            give[0, :, columns] = jnp.where(first, b, a)

        for q in range(NQ):
            block = total[:, q * QB : (q + 1) * QB]
            top = jnp.max(jnp.abs(block), axis=1, keepdims=True)
            scale = ((top + amax_eps) / quant_top).astype(bf16).astype(f32)
            store(block * (1.0 / scale), slice(q * QB, (q + 1) * QB))
            scales = jnp.where(lane == q, scale, scales)
        store(scales, slice(FF, WIDE))

    return pl.pallas_call(
        kernel,
        out_shape=[pltpu.HBM((NY, SHARD, WIDE), bf16)] * 2,
        grid_spec=pltpu.PrefetchScalarGridSpec(
            num_scalar_prefetch=1,
            grid=(NY,),
            in_specs=[pl.BlockSpec((a.shape[0], wide), lambda i, m: (0, i)) for a in flat]
            + [
                pl.BlockSpec((ALL_ROWS, FF), lambda i, m: (0, 0)),
                pl.BlockSpec((wide, FF), lambda i, m: (i, 0)),
            ],
            out_specs=[pl.BlockSpec((1, SHARD, WIDE), lambda i, m: (i, 0, 0))] * 2,
        ),
        compiler_params=params(1, 28),
        name="levels",
    )(me, *flat, ups, error)


def pair_sums(me, kept, given):
    part = 32

    def kernel(me_ref, a_ref, b_ref, *outs):
        y = me_ref[2]
        for k in range(NY):
            chip = lax.rem(y + k, NY)

            def rows(i, _):
                where = pl.ds(pl.multiple_of(i * part, part), part)
                sa = a_ref[chip, where, FF:].astype(f32)
                sb = b_ref[chip, where, FF:].astype(f32)
                for q in range(NQ):
                    columns = slice(q * QB, (q + 1) * QB)
                    total = (
                        a_ref[chip, where, columns].astype(f32) * sa[:, q : q + 1]
                        + b_ref[chip, where, columns].astype(f32) * sb[:, q : q + 1]
                    )
                    outs[k][where, columns] = total.astype(outs[k].dtype)
                return 0

            lax.fori_loop(0, SHARD // part, rows, 0)

    return pl.pallas_call(
        kernel,
        out_shape=[pltpu.VMEM((SHARD, FF), f32)] + [pltpu.VMEM((SHARD, FF), bf16)] * (NY - 1),
        in_specs=[SMEM_SPEC] + [VMEM_SPEC] * 2,
        out_specs=[VMEM_SPEC] * NY,
        compiler_params=params(mib=8),
        name="pair_sums",
    )(me, kept, given)


def adam(loss, sums, w, m, v):
    part = 32

    def kernel(loss_ref, *refs):
        got, (w_ref, m_ref, v_ref, nw_ref, nm_ref, nv_ref) = refs[:NY], refs[NY:]

        def rows(i, _):
            where = pl.ds(pl.multiple_of(i * part, part), part)
            total = got[0][where, :]
            for g in got[1:]:
                total = total + g[where, :].astype(f32)
            gradient = total / loss_ref[0]
            first = beta_one * m_ref[where, :].astype(f32) + (1.0 - beta_one) * gradient
            second = (
                beta_two * v_ref[where, :].astype(f32) + (1.0 - beta_two) * gradient * gradient
            )
            first_hat = first / (1.0 - beta_one**STEP)
            second_hat = second / (1.0 - beta_two**STEP)
            master = w_ref[where, :].astype(f32)
            updated = master - learn_rate * (
                first_hat / (jnp.sqrt(second_hat) + adam_eps) + decay_rate * master
            )
            nw_ref[where, :] = updated.astype(bf16)
            nm_ref[where, :] = first.astype(bf16)
            nv_ref[where, :] = second.astype(bf16)
            return 0

        lax.fori_loop(0, SHARD // part, rows, 0)

    return pl.pallas_call(
        kernel,
        out_shape=[pltpu.VMEM((SHARD, FF), bf16)]
        + [jax.ShapeDtypeStruct((SHARD, FF), bf16)] * 2,
        in_specs=[SMEM_SPEC] + [VMEM_SPEC] * (NY + 3),
        out_specs=[VMEM_SPEC] * 3,
        compiler_params=params(mib=8),
        name="adam",
    )(loss, *near(sums), w, m, v)


def assemble(me, same, other):
    def kernel(me_ref, *refs):
        shards, out, sems = refs[: 2 * NY], refs[2 * NY], refs[2 * NY + 1]
        y, core = me_ref[2], me_ref[3]
        copies = []
        for i, shard in enumerate(shards):
            k, owner = (i, core) if i < NY else (i - NY, 1 - core)
            place = lax.rem(y - k + NY, NY) * 2 + owner
            rows = pl.ds(pl.multiple_of(place * SHARD, SHARD), SHARD)
            copies.append(pltpu.make_async_copy(shard, out.at[0, rows, :], sems.at[i]))
        for copy in copies:
            copy.start()
        for copy in copies:
            copy.wait()

    return pl.pallas_call(
        kernel,
        out_shape=pltpu.HBM((1, D, FF), bf16),
        in_specs=[SMEM_SPEC] + [pl.BlockSpec(memory_space=pl.ANY)] * (2 * NY),
        out_specs=pl.BlockSpec(memory_space=pl.ANY),
        scratch_shapes=[pltpu.SemaphoreType.DMA((2 * NY,))],
        compiler_params=params(mib=2),
        name="assemble",
    )(me, *same, *other)


def step(tokens, routing, grad_up, up_shard, error_feedback, moment_one, moment_two, loss):
    def send(a, axis, n, shift):
        pairs = [(i, (i + shift) % n) for i in range(n)]
        return lax.ppermute(a, axis, pairs)

    def send_x(arrays, sign):
        return [arrays[0]] + [send(arrays[dx], "x", NX, sign * dx) for dx in range(1, NX)]

    def send_z(a, b):
        return send(a, "z", NZ, 1), send(b, "z", NZ, -1)

    def send_y(arrays):
        return [arrays[0]] + [send(arrays[k], "y", NY, k) for k in range(1, NY)]

    def swap(a):
        return lax.ppermute(a, "core", [(0, 1), (1, 0)])

    def gather(shard):
        same = send_y([shard] * NY)
        return same, [swap(same[k]) for k in range(NY)]

    me = jnp.stack([lax.axis_index(a) for a in ("x", "z", "y", "core")]).astype(jnp.int32)
    shards = jnp.broadcast_to(up_shard, (NY, SHARD, FF))
    same = lax.all_to_all(shards, "y", split_axis=0, concat_axis=0, tiled=True)
    other = swap(same)

    half = TOK // 2
    ext = prep(jnp.transpose(routing), tokens)
    block = {0: [ext]}
    up, down = ext, ext
    for r in (1, 2, 3):
        up, down = send_z(up, down)
        block[-r], block[r] = [up], [down]
    block[4] = list(send_z(up[:half], down[half:]))

    arrived, codes = [], []
    for offsets, rows in zip(CHUNKS, ROWS):
        out, code = dispatch(me, [block[o] for o in offsets], rows)
        arrived.append(send_x(out, 1))
        codes.append(code)
    hot = hots(codes[0:2], (0, 1)) + hots(codes[2:4], (2, 3)) + hots(codes[4:5], (4,))

    ups = ordered(me, grad_up[0])
    returned = slot_grads(me, ups, same, other)
    kept, given = levels_of(me, arrived, ups, error_feedback[0])
    sums = pair_sums(me, kept, swap(given))
    sums = send_y(sums)
    new_w, new_m, new_v = adam(loss.reshape(1), sums, up_shard[0], moment_one[0], moment_two[0])
    full = assemble(me, *gather(new_w))

    back = [None] * len(CHUNKS)
    for c in reversed(range(len(CHUNKS))):
        back[c] = send_x(returned[c], -1)
    top, low, whole = (0, half), (half, half), (0, TOK)
    u, d = combine(hot[4], back[4], [0], [[]], split=2)
    u, d = send_z(u, d)
    u, d = combine(hot[3], back[3], [1, 0], [[(u, top)], [(d, low)]])
    u, d = send_z(u, d)
    u, d = combine(hot[2], back[2], [1, 0], [[(u, whole)], [(d, whole)]])
    u, d = send_z(u, d)
    u, d = combine(hot[1], back[1], [1, 0], [[(u, whole)], [(d, whole)]])
    u, d = send_z(u, d)
    (grad_tokens,) = combine(hot[0], back[0], [0], [[(u, whole), (d, whole)]], last=True)
    return (grad_tokens, full, new_m[None], new_v[None])


def solution(mesh):
    fine = Mesh(mesh.devices.reshape(NX, NZ, NY, 2), ("x", "z", "y", "core"))
    expert = ("x", "z")
    in_specs = (
        P(("x", "z", "y", "core"), None),
        P(("x", "z", "y", "core"), None),
        P(expert, ("y", "core"), None),
        P(expert, ("y", "core"), None),
        P(expert, ("y", "core"), None),
        P(expert, ("y", "core"), None),
        P(expert, ("y", "core"), None),
        P(),
    )
    out_specs = (
        P(("x", "z", "y", "core"), None),
        P(expert, None, None),
        P(expert, ("y", "core"), None),
        P(expert, ("y", "core"), None),
    )
    return jax.shard_map(step, mesh=fine, in_specs=in_specs, out_specs=out_specs, check_vma=False)
```

```python
import jax
import jax.numpy as jnp
from jax import lax
from jax.experimental import pallas as pl
from jax.experimental.pallas import tpu as pltpu
from jax.sharding import Mesh, PartitionSpec as P

D = 2560
FF = 768
TOP = 6
QB = 128
NQ = FF // QB
STEP = 20
TOK = 128
CAP = 36
NX = 4
NZ = 8
NDP = 8
NY = 4
SHARD = D // NDP
INFO = 128
EXT = D + INFO
WIDE = FF + 128
TILE = 512

learn_rate = 0.001
beta_one = 0.9
beta_two = 0.999
decay_rate = 0.1
adam_eps = 1e-08
quant_top = 127.0
amax_eps = 1e-06

CHUNKS = ((0, -1, 1), (-2, 2), (-3, 3, 4))
ROWS = tuple(-(-len(c) * CAP // 8) * 8 for c in CHUNKS)
bf16 = jnp.bfloat16
f32 = jnp.float32


VMEM = pltpu.MemorySpace.VMEM
SMEM_SPEC = pl.BlockSpec(memory_space=pltpu.MemorySpace.SMEM)
VMEM_SPEC = pl.BlockSpec(memory_space=VMEM)
ALL_ROWS = NX * sum(ROWS)


def params(n=0, mib=6):
    if n == 0:
        return pltpu.CompilerParams(vmem_limit_bytes=mib << 20)
    return pltpu.CompilerParams(
        dimension_semantics=("arbitrary",) * n, vmem_limit_bytes=mib << 20
    )


def near(arrays):
    return [pltpu.with_memory_space_constraint(a, VMEM) for a in arrays]


def prep_kernel(routing_ref, tokens_ref, ext_ref):
    r = routing_ref[...]
    down = lax.broadcasted_iota(jnp.int32, (INFO, TOK), 0)
    across = lax.broadcasted_iota(jnp.int32, (INFO, TOK), 1)
    named = jnp.zeros((INFO, TOK), f32)
    for k in range(TOP):
        named = named + jnp.where(r[k : k + 1, :] == down, 1.0, 0.0)
    earlier = jnp.where(down < across, 1.0, 0.0).astype(bf16)
    before = jnp.dot(named.astype(bf16), earlier, preferred_element_type=f32)
    info = jnp.zeros((INFO, TOK), f32)
    for k in range(TOP):
        e = r[k : k + 1, :]
        w = jnp.sum(jnp.where(e == down, before, 0.0), axis=0, keepdims=True)
        info = jnp.where(down == k, e.astype(f32), info)
        info = jnp.where(down == TOP + k, w, info)
    ext_ref[:, :D] = tokens_ref[...]
    ext_ref[:, D:] = jnp.transpose(info).astype(bf16)


def prep(routing, tokens):
    return pl.pallas_call(
        prep_kernel,
        out_shape=pltpu.VMEM((TOK, EXT), bf16),
        in_specs=[VMEM_SPEC] * 2,
        out_specs=VMEM_SPEC,
        compiler_params=params(),
        name="prep",
    )(routing, tokens)


def stacked(parts):
    return jnp.concatenate([p.astype(f32) for p in parts], axis=0).astype(bf16)


def joined(parts):
    return parts[0] if len(parts) == 1 else jnp.concatenate(parts, axis=0)


def slot_of(e, w, x, z):
    ex = jnp.floor(e * 0.125)
    ez = e - ex * 8.0
    dx = ex - x
    dx = jnp.where(dx < 0.0, dx + float(NX), dx)
    return jnp.where(ez == z, dx * 64.0 + w, -1.0)


def placed(at, rows):
    side = jnp.floor((at + 0.5) * (1.0 / rows))
    return at - side * float(rows), side


def wanted(row, side, b):
    at = row - b * float(CAP)
    return jnp.where((at >= 0.0) & (at < float(CAP)), at + 64.0 * side, -2.0)


def dispatch(me, blocks, rows):
    nb = len(blocks)
    flat = [a for b in blocks for a in b]
    sizes = [len(b) for b in blocks]
    nf = len(flat)

    def kernel(me_ref, *refs):
        tok, outs, codes, hot = refs[:nf], refs[nf : nf + NX], refs[nf + NX], refs[-1]
        x = me_ref[0].astype(f32)
        z = me_ref[1].astype(f32)
        row = lax.broadcasted_iota(jnp.int32, (NX * rows, TOK), 0).astype(f32)
        row, side = placed(row, rows)
        at = 0
        for b in range(nb):
            raw = joined([t[:, D:] for t in tok[at : at + sizes[b]]]).astype(f32)
            at += sizes[b]
            codes[b * TOK : (b + 1) * TOK, :] = slot_of(
                raw, pltpu.roll(raw, INFO - TOP, 1), x, z
            ).astype(bf16)
            info = jnp.transpose(raw)
            code = slot_of(info[0:TOP], info[TOP : 2 * TOP], x, z)
            want = wanted(row, side, b)
            hit = jnp.zeros((NX * rows, TOK), f32)
            for k in range(TOP):
                hit = jnp.where(want == code[k : k + 1, :], 1.0, hit)
            hot[:, b * TOK : (b + 1) * TOK] = hit.astype(bf16)

        def column(i, _):
            where = pl.ds(pl.multiple_of(i * TILE, TILE), TILE)
            t = joined([t[:, where] for t in tok])
            got = jnp.dot(hot[...], t, preferred_element_type=f32)
            for dx in range(NX):
                outs[dx][:, where] = got[dx * rows : (dx + 1) * rows].astype(bf16)
            return 0

        lax.fori_loop(0, D // TILE, column, 0)

    out = pl.pallas_call(
        kernel,
        out_shape=[pltpu.VMEM((rows, D), bf16)] * NX
        + [jax.ShapeDtypeStruct((nb * TOK, INFO), bf16)],
        in_specs=[SMEM_SPEC] + [VMEM_SPEC] * nf,
        out_specs=[VMEM_SPEC] * (NX + 1),
        scratch_shapes=[pltpu.VMEM((NX * rows, nb * TOK), bf16)],
        compiler_params=params(),
        name="dispatch",
    )(me, *near(flat))
    return out[:NX], out[NX]


def hots(codes, chunks):
    nc = len(chunks)

    def kernel(*refs):
        for i, c in enumerate(chunks):
            codes_ref, out, rows = refs[i], refs[nc + i], ROWS[c]
            lane = lax.broadcasted_iota(jnp.int32, (TOK, NX * rows), 1).astype(f32)
            row, side = placed(lane, rows)

            def block(b, _):
                where = pl.ds(pl.multiple_of(b * TOK, TOK), TOK)
                code = codes_ref[where, :].astype(f32)
                want = wanted(row, side, lax.convert_element_type(b, f32))
                hit = jnp.zeros((TOK, NX * rows), f32)
                for k in range(TOP):
                    hit = jnp.where(want == code[:, k : k + 1], 1.0, hit)
                out[where, :] = hit.astype(bf16)
                return 0

            lax.fori_loop(0, len(CHUNKS[c]), block, 0)

    return pl.pallas_call(
        kernel,
        out_shape=[pltpu.VMEM((len(CHUNKS[c]) * TOK, NX * ROWS[c]), bf16) for c in chunks],
        in_specs=[VMEM_SPEC] * nc,
        out_specs=[VMEM_SPEC] * nc,
        compiler_params=params(),
        name="hots",
    )(*codes)


def combine(hot, rows_in, slots, adds, last=False, split=1):
    nb = len(slots)
    added = [a for p in adds for a, _ in p]
    na = len(added)

    def kernel(hot_ref, *refs):
        src, extra, outs = refs[:NX], refs[NX : NX + na], refs[NX + na :]

        def column(i, _):
            where = pl.ds(pl.multiple_of(i * TILE, TILE), TILE)
            data = stacked([s[:, where] for s in src])
            at = 0
            for b in range(nb):
                mine = jnp.dot(
                    hot_ref[slots[b] * TOK : (slots[b] + 1) * TOK, :],
                    data,
                    preferred_element_type=f32,
                )
                for _, (first, count) in adds[b]:
                    more = extra[at][:, where].astype(f32)
                    at += 1
                    if count < TOK:
                        pad = jnp.zeros((TOK - count, TILE), f32)
                        more = jnp.concatenate(
                            [more, pad] if first == 0 else [pad, more], axis=0
                        )
                    mine = mine + more
                mine = mine.astype(bf16)
                part = TOK // split
                for h in range(split):
                    outs[b * split + h][:, where] = mine[h * part : (h + 1) * part]
            return 0

        lax.fori_loop(0, D // TILE, column, 0)

    kind = (lambda s, t: jax.ShapeDtypeStruct(s, t)) if last else pltpu.VMEM
    return pl.pallas_call(
        kernel,
        out_shape=[kind((TOK // split, D), bf16)] * (nb * split),
        in_specs=[VMEM_SPEC] * (1 + NX + na),
        out_specs=[VMEM_SPEC] * (nb * split),
        compiler_params=params(),
        name="combine",
    )(*near([hot, *rows_in, *added]))


def order_kernel(me_ref, up_ref, out):
    x, z = me_ref[0], me_ref[1]
    picks = []
    for c, offsets in enumerate(CHUNKS):
        rows = ROWS[c]
        row = lax.broadcasted_iota(jnp.int32, (rows, NZ * CAP), 0)
        col = lax.broadcasted_iota(jnp.int32, (rows, NZ * CAP), 1)
        want = jnp.full((rows, NZ * CAP), -1, jnp.int32)
        for b, offset in enumerate(offsets):
            block = lax.rem(z + offset + NZ, NZ)
            inside = (row >= CAP * b) & (row < CAP * (b + 1))
            want = jnp.where(inside, block * CAP + row - CAP * b, want)
        picks.append(jnp.where(want == col, 1.0, 0.0).astype(bf16))

    def columns(i, _):
        where = pl.ds(pl.multiple_of(i * 256, 128), 256)
        got = []
        for pick in picks:
            for dx in range(NX):
                source = lax.rem(x - dx + NX, NX)
                start = pl.multiple_of(source * (NZ * CAP), 16)
                part = up_ref[pl.ds(start, NZ * CAP), where]
                got.append(jnp.dot(pick, part, preferred_element_type=f32))
        out[:, where] = jnp.concatenate(got, axis=0).astype(bf16)
        return 0

    lax.fori_loop(0, FF // 256, columns, 0)


def ordered(me, up):
    return pl.pallas_call(
        order_kernel,
        out_shape=jax.ShapeDtypeStruct((ALL_ROWS, FF), bf16),
        in_specs=[SMEM_SPEC, VMEM_SPEC],
        out_specs=VMEM_SPEC,
        compiler_params=params(),
        name="order",
    )(me, up)


def slot_grads(me, ups, same, other):
    flat_rows = [r for r in ROWS for _ in range(NX)]
    wide = 2 * SHARD

    def kernel(me_ref, up, mine, theirs, *outs):
        first = me_ref[3] == 0

        def chip(i, _):
            a, b = mine[i], theirs[i]
            w = jnp.concatenate([jnp.where(first, a, b), jnp.where(first, b, a)], axis=0)
            where = pl.ds(pl.multiple_of(i * wide, 128), wide)
            got = lax.dot_general(
                up[...], w, (((1,), (1,)), ((), ())), preferred_element_type=f32
            )
            at = 0
            for out, r in zip(outs, flat_rows):
                out[:, where] = got[at : at + r].astype(bf16)
                at += r
            return 0

        lax.fori_loop(0, NY, chip, 0)

    out = pl.pallas_call(
        kernel,
        out_shape=[pltpu.VMEM((r, D), bf16) for r in flat_rows],
        in_specs=[SMEM_SPEC] + [VMEM_SPEC] * 3,
        out_specs=[VMEM_SPEC] * len(flat_rows),
        compiler_params=params(mib=12),
        name="slot_grads",
    )(me, *near([ups, same, other]))
    return [out[c * NX : (c + 1) * NX] for c in range(len(ROWS))]


def products(src, up, where):
    slab = stacked([s[:, where] for s in src])
    return lax.dot_general(slab, up, (((0,), (0,)), ((), ())), preferred_element_type=f32)


def partial_of(rows_in, ups, error):
    flat = [a for c in rows_in for a in c]
    used = sum(a.shape[0] for a in flat)
    wide = 2 * SHARD

    def kernel(up, err, *refs):
        src, out = refs[:-1], refs[-1]

        def tile(i, _):
            where = pl.ds(pl.multiple_of(i * wide, 128), wide)
            out[where, :] = err[where, :].astype(f32) + products(src, up[:used, :], where)
            return 0

        lax.fori_loop(0, NY, tile, 0)

    return pl.pallas_call(
        kernel,
        out_shape=pltpu.VMEM((D, FF), f32),
        in_specs=[VMEM_SPEC] * (2 + len(flat)),
        out_specs=VMEM_SPEC,
        compiler_params=params(mib=12),
        name="partial",
    )(*near([ups, error, *flat]))


def levels_of(me, rows_in, ups, total):
    start = ALL_ROWS - sum(a.shape[0] for a in rows_in)
    wide = 2 * SHARD

    def kernel(me_ref, up, tot, *refs):
        src, (keep, give) = refs[:NX], refs[NX:]
        first = me_ref[3] == 0

        def tile(i, _):
            where = pl.ds(pl.multiple_of(i * wide, 128), wide)
            total = tot[where, :] + products(src, up[start:, :], where)
            lane = lax.broadcasted_iota(jnp.int32, (wide, QB), 1)
            scales = jnp.zeros((wide, QB), f32)

            def store(value, columns):
                a, b = value[:SHARD].astype(bf16), value[SHARD:].astype(bf16)
                keep[i, :, columns] = jnp.where(first, a, b)
                give[i, :, columns] = jnp.where(first, b, a)

            for q in range(NQ):
                block = total[:, q * QB : (q + 1) * QB]
                top = jnp.max(jnp.abs(block), axis=1, keepdims=True)
                scale = ((top + amax_eps) / quant_top).astype(bf16).astype(f32)
                store(block * (1.0 / scale), slice(q * QB, (q + 1) * QB))
                scales = jnp.where(lane == q, scale, scales)
            store(scales, slice(FF, WIDE))
            return 0

        lax.fori_loop(0, NY, tile, 0)

    return pl.pallas_call(
        kernel,
        out_shape=[pltpu.VMEM((NY, SHARD, WIDE), bf16)] * 2,
        in_specs=[SMEM_SPEC] + [VMEM_SPEC] * (2 + NX),
        out_specs=[VMEM_SPEC] * 2,
        compiler_params=params(mib=12),
        name="levels",
    )(me, *near([ups, total, *rows_in]))


def pair_sums(kept, given):
    def kernel(a_ref, b_ref, out):
        spread = (
            lax.broadcasted_iota(jnp.int32, (QB, FF), 0)
            == lax.broadcasted_iota(jnp.int32, (QB, FF), 1) // QB
        )
        spread = jnp.where(spread, 1.0, 0.0).astype(bf16)

        def chip(i, _):
            total = jnp.zeros((SHARD, FF), f32)
            for ref in (a_ref, b_ref):
                scale = jnp.dot(ref[i, :, FF:], spread, preferred_element_type=f32)
                total = total + ref[i, :, :FF].astype(f32) * scale
            out[i] = total.astype(bf16)
            return 0

        lax.fori_loop(0, NY, chip, 0)

    return pl.pallas_call(
        kernel,
        out_shape=pltpu.VMEM((NY, SHARD, FF), bf16),
        in_specs=[VMEM_SPEC] * 2,
        out_specs=VMEM_SPEC,
        compiler_params=params(mib=8),
        name="pair_sums",
    )(*near([kept, given]))


def adam(loss, sums, w, m, v):
    part = 32

    def kernel(loss_ref, got, w_ref, m_ref, v_ref, nw_ref, nm_ref, nv_ref):
        def rows(i, _):
            where = pl.ds(pl.multiple_of(i * part, part), part)
            total = got[0, where, :].astype(f32)
            for k in range(1, NY):
                total = total + got[k, where, :].astype(f32)
            gradient = total / loss_ref[0]
            first = beta_one * m_ref[where, :].astype(f32) + (1.0 - beta_one) * gradient
            second = (
                beta_two * v_ref[where, :].astype(f32) + (1.0 - beta_two) * gradient * gradient
            )
            first_hat = first / (1.0 - beta_one**STEP)
            second_hat = second / (1.0 - beta_two**STEP)
            master = w_ref[where, :].astype(f32)
            updated = master - learn_rate * (
                first_hat / (jnp.sqrt(second_hat) + adam_eps) + decay_rate * master
            )
            for k in range(NY):
                nw_ref[k, where, :] = updated.astype(bf16)
            nm_ref[where, :] = first.astype(bf16)
            nv_ref[where, :] = second.astype(bf16)
            return 0

        lax.fori_loop(0, SHARD // part, rows, 0)

    return pl.pallas_call(
        kernel,
        out_shape=[pltpu.VMEM((NY, SHARD, FF), bf16)]
        + [jax.ShapeDtypeStruct((SHARD, FF), bf16)] * 2,
        in_specs=[SMEM_SPEC] + [VMEM_SPEC] * 4,
        out_specs=[VMEM_SPEC] * 3,
        compiler_params=params(mib=8),
        name="adam",
    )(loss, *near([sums, w, m, v]))


def assemble(me, same, other):
    def kernel(me_ref, a_ref, b_ref, out, sems):
        core = me_ref[3]
        copies = []
        for i in range(2 * NY):
            shard, owner = (a_ref, core) if i < NY else (b_ref, 1 - core)
            place = (i % NY) * 2 + owner
            rows = pl.ds(pl.multiple_of(place * SHARD, SHARD), SHARD)
            copies.append(pltpu.make_async_copy(shard.at[i % NY], out.at[0, rows, :], sems.at[i]))
        for copy in copies:
            copy.start()
        for copy in copies:
            copy.wait()

    return pl.pallas_call(
        kernel,
        out_shape=pltpu.HBM((1, D, FF), bf16),
        in_specs=[SMEM_SPEC] + [pl.BlockSpec(memory_space=pl.ANY)] * 2,
        out_specs=pl.BlockSpec(memory_space=pl.ANY),
        scratch_shapes=[pltpu.SemaphoreType.DMA((2 * NY,))],
        compiler_params=params(mib=2),
        name="assemble",
    )(me, same, other)


def step(tokens, routing, grad_up, up_shard, error_feedback, moment_one, moment_two, loss):
    def send(a, axis, n, shift):
        pairs = [(i, (i + shift) % n) for i in range(n)]
        return lax.ppermute(a, axis, pairs)

    def send_x(arrays, sign):
        return [arrays[0]] + [send(arrays[dx], "x", NX, sign * dx) for dx in range(1, NX)]

    def send_z(a, b):
        return send(a, "z", NZ, 1), send(b, "z", NZ, -1)

    def send_y(a):
        return lax.all_to_all(a, "y", split_axis=0, concat_axis=0, tiled=True)

    def swap(a):
        return lax.ppermute(a, "core", [(0, 1), (1, 0)])

    def gather(shards):
        same = send_y(shards)
        return same, swap(same)

    me = jnp.stack([lax.axis_index(a) for a in ("x", "z", "y", "core")]).astype(jnp.int32)
    same, other = gather(jnp.broadcast_to(up_shard, (NY, SHARD, FF)))

    half = TOK // 2
    ext = prep(jnp.transpose(routing), tokens)
    block = {0: [ext]}
    up, down = ext, ext
    for r in (1, 2, 3):
        up, down = send_z(up, down)
        block[-r], block[r] = [up], [down]
    block[4] = list(send_z(up[:half], down[half:]))

    arrived, codes = [], []
    for offsets, rows in zip(CHUNKS, ROWS):
        out, code = dispatch(me, [block[o] for o in offsets], rows)
        arrived.append(send_x(out, 1))
        codes.append(code)
    hot = [hots(codes[c : c + 1], (c,))[0] for c in range(len(CHUNKS))]

    ups = ordered(me, grad_up[0])
    returned = slot_grads(me, ups, same, other)
    total = partial_of(arrived[:2], ups, error_feedback[0])
    kept, given = levels_of(me, arrived[2], ups, total)
    sums = pair_sums(kept, swap(given))
    sums = send_y(sums)
    new_w, new_m, new_v = adam(loss.reshape(1), sums, up_shard[0], moment_one[0], moment_two[0])
    full = assemble(me, *gather(new_w))

    back = [None] * len(CHUNKS)
    for c in reversed(range(len(CHUNKS))):
        back[c] = send_x(returned[c], -1)
    top, low, whole = (0, half), (half, half), (0, TOK)
    u, d = combine(hot[2], back[2], [2], [[]], split=2)
    u, d = send_z(u, d)
    u, d = combine(hot[2], back[2], [1, 0], [[(u, top)], [(d, low)]])
    u, d = send_z(u, d)
    u, d = combine(hot[1], back[1], [1, 0], [[(u, whole)], [(d, whole)]])
    u, d = send_z(u, d)
    u, d = combine(hot[0], back[0], [2, 1], [[(u, whole)], [(d, whole)]])
    u, d = send_z(u, d)
    (grad_tokens,) = combine(hot[0], back[0], [0], [[(u, whole), (d, whole)]], last=True)
    return (grad_tokens, full, new_m[None], new_v[None])


def solution(mesh):
    fine = Mesh(mesh.devices.reshape(NX, NZ, NY, 2), ("x", "z", "y", "core"))
    expert = ("x", "z")
    in_specs = (
        P(("x", "z", "y", "core"), None),
        P(("x", "z", "y", "core"), None),
        P(expert, ("y", "core"), None),
        P(expert, ("y", "core"), None),
        P(expert, ("y", "core"), None),
        P(expert, ("y", "core"), None),
        P(expert, ("y", "core"), None),
        P(),
    )
    out_specs = (
        P(("x", "z", "y", "core"), None),
        P(expert, None, None),
        P(expert, ("y", "core"), None),
        P(expert, ("y", "core"), None),
    )
    return jax.shard_map(step, mesh=fine, in_specs=in_specs, out_specs=out_specs, check_vma=False)
```

```python
import jax
import jax.numpy as jnp
from jax import lax
from jax.experimental import pallas as pl
from jax.experimental.pallas import tpu as pltpu
from jax.sharding import Mesh, PartitionSpec as P

D = 2560
FF = 768
TOP = 6
QB = 128
NQ = FF // QB
STEP = 20
TOK = 128
CAP = 36
NX = 4
NZ = 8
NDP = 8
NY = 4
SHARD = D // NDP
INFO = 128
EXT = D + INFO
WIDE = FF + 128
TILE = 512

learn_rate = 0.001
beta_one = 0.9
beta_two = 0.999
decay_rate = 0.1
adam_eps = 1e-08
quant_top = 127.0
amax_eps = 1e-06

CHUNKS = ((0, -1, 1), (-2, 2), (-3, 3, 4))
ROWS = tuple(-(-len(c) * CAP // 8) * 8 for c in CHUNKS)
BACK = {0: (0, 0, 3, 0, 112), 2: (1, 0, 2, 0, 72), 3: (2, 0, 2, 0, 72), 4: (2, 2, 1, 72, 40)}
bf16 = jnp.bfloat16
f32 = jnp.float32


VMEM = pltpu.MemorySpace.VMEM
SMEM_SPEC = pl.BlockSpec(memory_space=pltpu.MemorySpace.SMEM)
VMEM_SPEC = pl.BlockSpec(memory_space=VMEM)
STARTS = tuple(NX * sum(ROWS[:c]) for c in range(len(ROWS)))
ALL_ROWS = NX * sum(ROWS)


def params(n=0, mib=6):
    if n == 0:
        return pltpu.CompilerParams(vmem_limit_bytes=mib << 20)
    return pltpu.CompilerParams(
        dimension_semantics=("arbitrary",) * n, vmem_limit_bytes=mib << 20
    )


def near(arrays):
    return [pltpu.with_memory_space_constraint(a, VMEM) for a in arrays]


def far(arrays):
    return [pltpu.with_memory_space_constraint(a, pltpu.MemorySpace.HBM) for a in arrays]


def prep_kernel(routing_ref, tokens_ref, ext_ref):
    r = routing_ref[...]
    down = lax.broadcasted_iota(jnp.int32, (INFO, TOK), 0)
    across = lax.broadcasted_iota(jnp.int32, (INFO, TOK), 1)
    named = jnp.zeros((INFO, TOK), f32)
    for k in range(TOP):
        named = named + jnp.where(r[k : k + 1, :] == down, 1.0, 0.0)
    earlier = jnp.where(down < across, 1.0, 0.0).astype(bf16)
    before = jnp.dot(named.astype(bf16), earlier, preferred_element_type=f32)
    info = jnp.zeros((INFO, TOK), f32)
    for k in range(TOP):
        e = r[k : k + 1, :]
        w = jnp.sum(jnp.where(e == down, before, 0.0), axis=0, keepdims=True)
        info = jnp.where(down == k, e.astype(f32), info)
        info = jnp.where(down == TOP + k, w, info)
    ext_ref[:, :D] = tokens_ref[...]
    ext_ref[:, D:] = jnp.transpose(info).astype(bf16)


def prep(routing, tokens):
    return pl.pallas_call(
        prep_kernel,
        out_shape=pltpu.VMEM((TOK, EXT), bf16),
        in_specs=[VMEM_SPEC] * 2,
        out_specs=VMEM_SPEC,
        compiler_params=params(),
        name="prep",
    )(routing, tokens)


def stacked(parts):
    if all(p.shape[0] % 16 == 0 for p in parts):
        return jnp.concatenate(parts, axis=0)
    return jnp.concatenate([p.astype(f32) for p in parts], axis=0).astype(bf16)


def joined(parts):
    return parts[0] if len(parts) == 1 else jnp.concatenate(parts, axis=0)


def slot_of(e, w, x, z):
    ex = jnp.floor(e * 0.125)
    ez = e - ex * 8.0
    dx = ex - x
    dx = jnp.where(dx < 0.0, dx + float(NX), dx)
    return jnp.where(ez == z, dx * 64.0 + w, -1.0)


def placed(at, rows):
    side = jnp.floor((at + 0.5) * (1.0 / rows))
    return at - side * float(rows), side


def wanted(row, side, b):
    at = row - b * float(CAP)
    return jnp.where((at >= 0.0) & (at < float(CAP)), at + 64.0 * side, -2.0)


def dispatch(me, blocks, rows):
    nb = len(blocks)
    flat = [a for b in blocks for a in b]
    sizes = [len(b) for b in blocks]
    nf = len(flat)
    high = -(-rows // 16) * 16

    def kernel(me_ref, *refs):
        tok, outs = refs[:nf], refs[nf : nf + NX]
        codes, hot, code = refs[nf + NX :]
        x = me_ref[0].astype(f32)
        z = me_ref[1].astype(f32)
        row = lax.broadcasted_iota(jnp.int32, (high, TOK), 0).astype(f32)
        at = 0
        for b in range(nb):
            raw = joined([t[:, D:] for t in tok[at : at + sizes[b]]]).astype(f32)
            at += sizes[b]
            codes[b * TOK : (b + 1) * TOK, :] = slot_of(
                raw, pltpu.roll(raw, INFO - TOP, 1), x, z
            ).astype(bf16)
            info = jnp.transpose(raw)
            code[8 * b : 8 * b + TOP, :] = slot_of(info[0:TOP], info[TOP : 2 * TOP], x, z)

        def side(dx, _):
            for b in range(nb):
                want = wanted(row, lax.convert_element_type(dx, f32), b)
                hit = jnp.zeros((high, TOK), f32)
                for k in range(TOP):
                    hit = jnp.where(want == code[8 * b + k : 8 * b + k + 1, :], 1.0, hit)
                where = pl.ds(pl.multiple_of(dx * high, 16), high)
                hot[where, b * TOK : (b + 1) * TOK] = hit.astype(bf16)
            return 0

        lax.fori_loop(0, NX, side, 0)

        def column(i, _):
            where = pl.ds(pl.multiple_of(i * TILE, TILE), TILE)
            t = joined([t[:, where] for t in tok])
            got = jnp.dot(hot[...], t, preferred_element_type=f32)
            for dx in range(NX):
                outs[dx][:, where] = got[dx * high : dx * high + rows].astype(bf16)
            return 0

        lax.fori_loop(0, D // TILE, column, 0)

    out = pl.pallas_call(
        kernel,
        out_shape=[pltpu.VMEM((rows, D), bf16)] * NX
        + [jax.ShapeDtypeStruct((nb * TOK, INFO), bf16)],
        in_specs=[SMEM_SPEC] + [VMEM_SPEC] * nf,
        out_specs=[VMEM_SPEC] * (NX + 1),
        scratch_shapes=[pltpu.VMEM((NX * high, nb * TOK), bf16), pltpu.VMEM((8 * nb, TOK), f32)],
        compiler_params=params(),
        name="dispatch",
    )(me, *near(flat))
    return out[:NX], out[NX]


def hots(codes, piece):
    _, start, blocks, _, rows = BACK[piece]

    def kernel(codes_ref, out):
        lane = lax.broadcasted_iota(jnp.int32, (TOK, NX * rows), 1).astype(f32)
        row, side = placed(lane, rows)

        def block(b, _):
            where = pl.ds(pl.multiple_of((start + b) * TOK, TOK), TOK)
            code = codes_ref[where, :].astype(f32)
            want = wanted(row, side, lax.convert_element_type(b, f32))
            hit = jnp.zeros((TOK, NX * rows), f32)
            for k in range(TOP):
                hit = jnp.where(want == code[:, k : k + 1], 1.0, hit)
            out[pl.ds(pl.multiple_of(b * TOK, TOK), TOK), :] = hit.astype(bf16)
            return 0

        lax.fori_loop(0, blocks, block, 0)

    return pl.pallas_call(
        kernel,
        out_shape=pltpu.VMEM((blocks * TOK, NX * rows), bf16),
        in_specs=[VMEM_SPEC],
        out_specs=VMEM_SPEC,
        compiler_params=params(),
        name="hots",
    )(codes)


def combine(hot, rows_in, slots, adds, last=False, split=1):
    nb = len(slots)
    added = [a for p in adds for a, _ in p]
    na = len(added)

    def kernel(hot_ref, *refs):
        src, extra, outs = refs[:NX], refs[NX : NX + na], refs[NX + na :]

        def column(i, _):
            where = pl.ds(pl.multiple_of(i * TILE, TILE), TILE)
            data = stacked([s[:, where] for s in src])
            at = 0
            for b in range(nb):
                mine = jnp.dot(
                    hot_ref[slots[b] * TOK : (slots[b] + 1) * TOK, :],
                    data,
                    preferred_element_type=f32,
                )
                for _, (first, count) in adds[b]:
                    more = extra[at][:, where].astype(f32)
                    at += 1
                    if count < TOK:
                        pad = jnp.zeros((TOK - count, TILE), f32)
                        more = jnp.concatenate(
                            [more, pad] if first == 0 else [pad, more], axis=0
                        )
                    mine = mine + more
                mine = mine.astype(bf16)
                part = TOK // split
                for h in range(split):
                    outs[b * split + h][:, where] = mine[h * part : (h + 1) * part]
            return 0

        lax.fori_loop(0, D // TILE, column, 0)

    kind = (lambda s, t: jax.ShapeDtypeStruct(s, t)) if last else pltpu.VMEM
    return pl.pallas_call(
        kernel,
        out_shape=[kind((TOK // split, D), bf16)] * (nb * split),
        in_specs=[VMEM_SPEC] * (1 + NX + na),
        out_specs=[VMEM_SPEC] * (nb * split),
        compiler_params=params(),
        name="combine",
    )(*near([hot, *rows_in, *added]))


def order_kernel(me_ref, loss_ref, up_ref, out, loss_out):
    loss_out[...] = jnp.full((8, FF), loss_ref[0], f32)
    x, z = me_ref[0], me_ref[1]
    picks = []
    for c, offsets in enumerate(CHUNKS):
        rows = ROWS[c]
        row = lax.broadcasted_iota(jnp.int32, (rows, NZ * CAP), 0)
        col = lax.broadcasted_iota(jnp.int32, (rows, NZ * CAP), 1)
        want = jnp.full((rows, NZ * CAP), -1, jnp.int32)
        for b, offset in enumerate(offsets):
            block = lax.rem(z + offset + NZ, NZ)
            inside = (row >= CAP * b) & (row < CAP * (b + 1))
            want = jnp.where(inside, block * CAP + row - CAP * b, want)
        picks.append(jnp.where(want == col, 1.0, 0.0).astype(bf16))

    def columns(i, _):
        where = pl.ds(pl.multiple_of(i * 256, 128), 256)
        got = []
        for pick in picks:
            for dx in range(NX):
                source = lax.rem(x - dx + NX, NX)
                start = pl.multiple_of(source * (NZ * CAP), 16)
                part = up_ref[pl.ds(start, NZ * CAP), where]
                got.append(jnp.dot(pick, part, preferred_element_type=f32))
        out[:, where] = jnp.concatenate(got, axis=0).astype(bf16)
        return 0

    lax.fori_loop(0, FF // 256, columns, 0)


def ordered(me, loss, up):
    return pl.pallas_call(
        order_kernel,
        out_shape=[
            jax.ShapeDtypeStruct((ALL_ROWS, FF), bf16),
            jax.ShapeDtypeStruct((8, FF), f32),
        ],
        in_specs=[SMEM_SPEC, SMEM_SPEC, VMEM_SPEC],
        out_specs=[VMEM_SPEC] * 2,
        compiler_params=params(),
        name="order",
    )(me, loss.reshape(1), up)


def slot_grads(me, ups, same, other):
    order = sorted(BACK)
    flat = [(p, dx) for p in order for dx in range(NX)]
    wide = 2 * SHARD

    def kernel(me_ref, up, mine, theirs, *outs):
        first = me_ref[3] == 0

        def chip(i, _):
            a, b = mine[i], theirs[i]
            w = jnp.concatenate([jnp.where(first, a, b), jnp.where(first, b, a)], axis=0)
            where = pl.ds(pl.multiple_of(i * wide, 128), wide)
            got = lax.dot_general(
                up[...], w, (((1,), (1,)), ((), ())), preferred_element_type=f32
            )
            for out, (p, dx) in zip(outs, flat):
                c, _, _, start, rows = BACK[p]
                at = STARTS[c] + dx * ROWS[c] + start
                out[:, where] = got[at : at + rows].astype(bf16)
            return 0

        lax.fori_loop(0, NY, chip, 0)

    out = pl.pallas_call(
        kernel,
        out_shape=[pltpu.VMEM((BACK[p][4], D), bf16) for p, _ in flat],
        in_specs=[SMEM_SPEC] + [VMEM_SPEC] * 3,
        out_specs=[VMEM_SPEC] * len(flat),
        compiler_params=params(mib=12),
        name="slot_grads",
    )(me, *near([ups, same, other]))
    return {p: out[i * NX : (i + 1) * NX] for i, p in enumerate(order)}


def products(src, up, where):
    slab = stacked([s[:, where] for s in src])
    return lax.dot_general(slab, up, (((0,), (0,)), ((), ())), preferred_element_type=f32)


def partial_of(rows_in, ups, error):
    flat = [a for c in rows_in for a in c]
    used = sum(a.shape[0] for a in flat)
    wide = 2 * SHARD

    def kernel(up, err, *refs):
        src, out = refs[:-1], refs[-1]

        def tile(i, _):
            where = pl.ds(pl.multiple_of(i * wide, 128), wide)
            out[where, :] = err[where, :].astype(f32) + products(src, up[:used, :], where)
            return 0

        lax.fori_loop(0, NY, tile, 0)

    return pl.pallas_call(
        kernel,
        out_shape=pltpu.VMEM((D, FF), f32),
        in_specs=[VMEM_SPEC] * (2 + len(flat)),
        out_specs=VMEM_SPEC,
        compiler_params=params(mib=12),
        name="partial",
    )(*near([ups, error, *flat]))


def levels_of(me, rows_in, ups, total):
    start = ALL_ROWS - sum(a.shape[0] for a in rows_in)
    wide = 2 * SHARD

    def kernel(me_ref, up, tot, *refs):
        src, (keep, give) = refs[:NX], refs[NX:]
        first = me_ref[3] == 0

        def tile(i, _):
            where = pl.ds(pl.multiple_of(i * wide, 128), wide)
            total = tot[where, :] + products(src, up[start:, :], where)
            lane = lax.broadcasted_iota(jnp.int32, (wide, QB), 1)
            scales = jnp.zeros((wide, QB), f32)

            def store(value, columns):
                a, b = value[:SHARD].astype(bf16), value[SHARD:].astype(bf16)
                keep[i, :, columns] = jnp.where(first, a, b)
                give[i, :, columns] = jnp.where(first, b, a)

            for q in range(NQ):
                block = total[:, q * QB : (q + 1) * QB]
                top = jnp.max(jnp.abs(block), axis=1, keepdims=True)
                scale = ((top + amax_eps) / quant_top).astype(bf16).astype(f32)
                store(block * (1.0 / scale), slice(q * QB, (q + 1) * QB))
                scales = jnp.where(lane == q, scale, scales)
            store(scales, slice(FF, WIDE))
            return 0

        lax.fori_loop(0, NY, tile, 0)

    return pl.pallas_call(
        kernel,
        out_shape=[pltpu.VMEM((NY, SHARD, WIDE), bf16)] * 2,
        in_specs=[SMEM_SPEC] + [VMEM_SPEC] * (2 + NX),
        out_specs=[VMEM_SPEC] * 2,
        compiler_params=params(mib=12),
        name="levels",
    )(me, *near([ups, total, *rows_in]))


def pair_sums(me, kept, given):
    def kernel(me_ref, a_ref, b_ref, *outs):
        y = me_ref[2]
        spread = (
            lax.broadcasted_iota(jnp.int32, (QB, FF), 0)
            == lax.broadcasted_iota(jnp.int32, (QB, FF), 1) // QB
        )
        spread = jnp.where(spread, 1.0, 0.0).astype(bf16)
        for k in range(NY):
            chip = lax.rem(y + k, NY)
            total = jnp.zeros((SHARD, FF), f32)
            for ref in (a_ref, b_ref):
                scale = jnp.dot(ref[chip, :, FF:], spread, preferred_element_type=f32)
                total = total + ref[chip, :, :FF].astype(f32) * scale
            outs[k][...] = total.astype(bf16)

    return pl.pallas_call(
        kernel,
        out_shape=[pltpu.VMEM((SHARD, FF), bf16)] * NY,
        in_specs=[SMEM_SPEC] + [VMEM_SPEC] * 2,
        out_specs=[VMEM_SPEC] * NY,
        compiler_params=params(mib=8),
        name="pair_sums",
    )(me, *near([kept, given]))


def adam(loss, sums, w, m, v):
    part = 32

    def kernel(loss_ref, *refs):
        got, (w_ref, m_ref, v_ref, nw_ref, nm_ref, nv_ref) = refs[:NY], refs[NY:]

        def rows(i, _):
            where = pl.ds(pl.multiple_of(i * part, part), part)
            total = got[0][where, :].astype(f32)
            for g in got[1:]:
                total = total + g[where, :].astype(f32)
            gradient = total / loss_ref[0:1, :]
            first = beta_one * m_ref[where, :].astype(f32) + (1.0 - beta_one) * gradient
            second = (
                beta_two * v_ref[where, :].astype(f32) + (1.0 - beta_two) * gradient * gradient
            )
            first_hat = first / (1.0 - beta_one**STEP)
            second_hat = second / (1.0 - beta_two**STEP)
            master = w_ref[where, :].astype(f32)
            updated = master - learn_rate * (
                first_hat / (jnp.sqrt(second_hat) + adam_eps) + decay_rate * master
            )
            nw_ref[where, :] = updated.astype(bf16)
            nm_ref[where, :] = first.astype(bf16)
            nv_ref[where, :] = second.astype(bf16)
            return 0

        lax.fori_loop(0, SHARD // part, rows, 0)

    return pl.pallas_call(
        kernel,
        out_shape=[pltpu.VMEM((SHARD, FF), bf16)]
        + [jax.ShapeDtypeStruct((SHARD, FF), bf16)] * 2,
        in_specs=[VMEM_SPEC] * (NY + 4),
        out_specs=[VMEM_SPEC] * 3,
        compiler_params=params(mib=8),
        name="adam",
    )(loss, *near(sums), *far([w, m, v]))


def assemble(me, same, other):
    def kernel(me_ref, *refs):
        shards, out, sems = refs[: 2 * NY], refs[2 * NY], refs[2 * NY + 1]
        y, core = me_ref[2], me_ref[3]
        copies = []
        for i, shard in enumerate(shards):
            owner = core if i < NY else 1 - core
            place = lax.rem(y - i % NY + NY, NY) * 2 + owner
            rows = pl.ds(pl.multiple_of(place * SHARD, SHARD), SHARD)
            copies.append(pltpu.make_async_copy(shard, out.at[0, rows, :], sems.at[i]))
        for copy in copies:
            copy.start()
        for copy in copies:
            copy.wait()

    return pl.pallas_call(
        kernel,
        out_shape=pltpu.HBM((1, D, FF), bf16),
        in_specs=[SMEM_SPEC] + [pl.BlockSpec(memory_space=pl.ANY)] * (2 * NY),
        out_specs=pl.BlockSpec(memory_space=pl.ANY),
        scratch_shapes=[pltpu.SemaphoreType.DMA((2 * NY,))],
        compiler_params=params(mib=2),
        name="assemble",
    )(me, *same, *other)


def step(tokens, routing, grad_up, up_shard, error_feedback, moment_one, moment_two, loss):
    def send(a, axis, n, shift):
        pairs = [(i, (i + shift) % n) for i in range(n)]
        return lax.ppermute(a, axis, pairs)

    def send_x(arrays, sign):
        return [arrays[0]] + [send(arrays[dx], "x", NX, sign * dx) for dx in range(1, NX)]

    def send_z(a, b):
        return send(a, "z", NZ, 1), send(b, "z", NZ, -1)

    def send_y(arrays):
        return [arrays[0]] + [send(arrays[k], "y", NY, k) for k in range(1, NY)]

    def swap(a):
        return lax.ppermute(a, "core", [(0, 1), (1, 0)])

    me = jnp.stack([lax.axis_index(a) for a in ("x", "z", "y", "core")]).astype(jnp.int32)
    same = jnp.broadcast_to(up_shard, (NY, SHARD, FF))
    same = lax.all_to_all(same, "y", split_axis=0, concat_axis=0, tiled=True)
    other = swap(same)

    half = TOK // 2
    ext = prep(jnp.transpose(routing), tokens)
    block = {0: [ext]}
    up, down = ext, ext
    for r in (1, 2, 3):
        up, down = send_z(up, down)
        block[-r], block[r] = [up], [down]
    block[4] = list(send_z(up[:half], down[half:]))

    arrived, codes = [], []
    for offsets, rows in zip(CHUNKS, ROWS):
        out, code = dispatch(me, [block[o] for o in offsets], rows)
        arrived.append(send_x(out, 1))
        codes.append(code)
    hot = {p: hots(codes[BACK[p][0]], p) for p in BACK}

    ups, loss_row = ordered(me, loss, grad_up[0])
    returned = slot_grads(me, ups, same, other)
    total = partial_of(arrived[:2], ups, error_feedback[0])
    kept, given = levels_of(me, arrived[2], ups, total)
    sums = pair_sums(me, kept, swap(given))
    sums = send_y(sums)
    new_w, new_m, new_v = adam(loss_row, sums, up_shard[0], moment_one[0], moment_two[0])
    shards = send_y([new_w] * NY)
    full = assemble(me, shards, [swap(a) for a in shards])

    back = {p: send_x(returned[p], -1) for p in (4, 3, 2, 0)}
    top, low, whole = (0, half), (half, half), (0, TOK)
    u, d = combine(hot[4], back[4], [0], [[]], split=2)
    u, d = send_z(u, d)
    u, d = combine(hot[3], back[3], [1, 0], [[(u, top)], [(d, low)]])
    u, d = send_z(u, d)
    u, d = combine(hot[2], back[2], [1, 0], [[(u, whole)], [(d, whole)]])
    u, d = send_z(u, d)
    u, d = combine(hot[0], back[0], [2, 1], [[(u, whole)], [(d, whole)]])
    u, d = send_z(u, d)
    (grad_tokens,) = combine(hot[0], back[0], [0], [[(u, whole), (d, whole)]], last=True)
    return (grad_tokens, full, new_m[None], new_v[None])


def solution(mesh):
    fine = Mesh(mesh.devices.reshape(NX, NZ, NY, 2), ("x", "z", "y", "core"))
    expert = ("x", "z")
    in_specs = (
        P(("x", "z", "y", "core"), None),
        P(("x", "z", "y", "core"), None),
        P(expert, ("y", "core"), None),
        P(expert, ("y", "core"), None),
        P(expert, ("y", "core"), None),
        P(expert, ("y", "core"), None),
        P(expert, ("y", "core"), None),
        P(),
    )
    out_specs = (
        P(("x", "z", "y", "core"), None),
        P(expert, None, None),
        P(expert, ("y", "core"), None),
        P(expert, ("y", "core"), None),
    )
    return jax.shard_map(step, mesh=fine, in_specs=in_specs, out_specs=out_specs, check_vma=False)
```

```python
import jax
import jax.numpy as jnp
from jax import lax
from jax.experimental import pallas as pl
from jax.experimental.pallas import tpu as pltpu
from jax.sharding import Mesh, PartitionSpec as P

D = 2560
FF = 768
TOP = 6
QB = 128
NQ = FF // QB
STEP = 20
TOK = 128
CAP = 36
NX = 4
NZ = 8
NDP = 8
NY = 4
SHARD = D // NDP
INFO = 128
EXT = D + INFO
WIDE = FF + 128
TILE = 512

learn_rate = 0.001
beta_one = 0.9
beta_two = 0.999
decay_rate = 0.1
adam_eps = 1e-08
quant_top = 127.0
amax_eps = 1e-06

CHUNKS = ((0, -1, 1), (-2, 2), (-3, 3, 4))
ROWS = tuple(-(-len(c) * CAP // 8) * 8 for c in CHUNKS)
BACK = {0: (0, 0, 3, 0, 112), 2: (1, 0, 2, 0, 72), 3: (2, 0, 2, 0, 72), 4: (2, 2, 1, 72, 40)}
bf16 = jnp.bfloat16
f32 = jnp.float32


VMEM = pltpu.MemorySpace.VMEM
SMEM_SPEC = pl.BlockSpec(memory_space=pltpu.MemorySpace.SMEM)
VMEM_SPEC = pl.BlockSpec(memory_space=VMEM)
STARTS = tuple(NX * sum(ROWS[:c]) for c in range(len(ROWS)))
ALL_ROWS = NX * sum(ROWS)


def params(n=0, mib=6):
    if n == 0:
        return pltpu.CompilerParams(vmem_limit_bytes=mib << 20)
    return pltpu.CompilerParams(
        dimension_semantics=("arbitrary",) * n, vmem_limit_bytes=mib << 20
    )


def near(arrays):
    return [pltpu.with_memory_space_constraint(a, VMEM) for a in arrays]


def far(arrays):
    return [pltpu.with_memory_space_constraint(a, pltpu.MemorySpace.HBM) for a in arrays]


def prep_kernel(routing_ref, tokens_ref, ext_ref):
    r = routing_ref[...]
    down = lax.broadcasted_iota(jnp.int32, (INFO, TOK), 0)
    across = lax.broadcasted_iota(jnp.int32, (INFO, TOK), 1)
    named = jnp.zeros((INFO, TOK), f32)
    for k in range(TOP):
        named = named + jnp.where(r[k : k + 1, :] == down, 1.0, 0.0)
    earlier = jnp.where(down < across, 1.0, 0.0).astype(bf16)
    before = jnp.dot(named.astype(bf16), earlier, preferred_element_type=f32)
    info = jnp.zeros((INFO, TOK), f32)
    for k in range(TOP):
        e = r[k : k + 1, :]
        w = jnp.sum(jnp.where(e == down, before, 0.0), axis=0, keepdims=True)
        info = jnp.where(down == k, e.astype(f32), info)
        info = jnp.where(down == TOP + k, w, info)
    ext_ref[:, :D] = tokens_ref[...]
    ext_ref[:, D:] = jnp.transpose(info).astype(bf16)


def prep(routing, tokens):
    return pl.pallas_call(
        prep_kernel,
        out_shape=pltpu.VMEM((TOK, EXT), bf16),
        in_specs=[VMEM_SPEC] * 2,
        out_specs=VMEM_SPEC,
        compiler_params=params(),
        name="prep",
    )(routing, tokens)


def stacked(parts):
    if all(p.shape[0] % 16 == 0 for p in parts):
        return jnp.concatenate(parts, axis=0)
    return jnp.concatenate([p.astype(f32) for p in parts], axis=0).astype(bf16)


def joined(parts):
    return parts[0] if len(parts) == 1 else jnp.concatenate(parts, axis=0)


def slot_of(e, w, x, z):
    ex = jnp.floor(e * 0.125)
    ez = e - ex * 8.0
    dx = ex - x
    dx = jnp.where(dx < 0.0, dx + float(NX), dx)
    return jnp.where(ez == z, dx * 64.0 + w, -1.0)


def placed(at, rows):
    side = jnp.floor((at + 0.5) * (1.0 / rows))
    return at - side * float(rows), side


def wanted(row, side, b):
    at = row - b * float(CAP)
    return jnp.where((at >= 0.0) & (at < float(CAP)), at + 64.0 * side, -2.0)


def dispatch(me, blocks, rows):
    nb = len(blocks)
    flat = [a for b in blocks for a in b]
    sizes = [len(b) for b in blocks]
    nf = len(flat)
    high = -(-rows // 16) * 16

    def kernel(me_ref, *refs):
        tok, outs = refs[:nf], refs[nf : nf + NX]
        codes, hot, code = refs[nf + NX :]
        x = me_ref[0].astype(f32)
        z = me_ref[1].astype(f32)
        row = lax.broadcasted_iota(jnp.int32, (high, TOK), 0).astype(f32)
        at = 0
        for b in range(nb):
            raw = joined([t[:, D:] for t in tok[at : at + sizes[b]]]).astype(f32)
            at += sizes[b]
            codes[b * TOK : (b + 1) * TOK, :] = slot_of(
                raw, pltpu.roll(raw, INFO - TOP, 1), x, z
            ).astype(bf16)
            info = jnp.transpose(raw)
            code[8 * b : 8 * b + TOP, :] = slot_of(info[0:TOP], info[TOP : 2 * TOP], x, z)

        def side(dx, _):
            for b in range(nb):
                want = wanted(row, lax.convert_element_type(dx, f32), b)
                hit = jnp.zeros((high, TOK), f32)
                for k in range(TOP):
                    hit = jnp.where(want == code[8 * b + k : 8 * b + k + 1, :], 1.0, hit)
                where = pl.ds(pl.multiple_of(dx * high, 16), high)
                hot[where, b * TOK : (b + 1) * TOK] = hit.astype(bf16)
            return 0

        lax.fori_loop(0, NX, side, 0)

        def column(i, _):
            where = pl.ds(pl.multiple_of(i * TILE, TILE), TILE)
            t = joined([t[:, where] for t in tok])
            got = jnp.dot(hot[...], t, preferred_element_type=f32)
            for dx in range(NX):
                outs[dx][:, where] = got[dx * high : dx * high + rows].astype(bf16)
            return 0

        lax.fori_loop(0, D // TILE, column, 0)

    out = pl.pallas_call(
        kernel,
        out_shape=[pltpu.VMEM((rows, D), bf16)] * NX
        + [jax.ShapeDtypeStruct((nb * TOK, INFO), bf16)],
        in_specs=[SMEM_SPEC] + [VMEM_SPEC] * nf,
        out_specs=[VMEM_SPEC] * (NX + 1),
        scratch_shapes=[pltpu.VMEM((NX * high, nb * TOK), bf16), pltpu.VMEM((8 * nb, TOK), f32)],
        compiler_params=params(),
        name="dispatch",
    )(me, *near(flat))
    return out[:NX], out[NX]


def hots(codes, piece):
    _, start, blocks, _, rows = BACK[piece]

    def kernel(codes_ref, out):
        lane = lax.broadcasted_iota(jnp.int32, (TOK, NX * rows), 1).astype(f32)
        row, side = placed(lane, rows)

        def block(b, _):
            where = pl.ds(pl.multiple_of((start + b) * TOK, TOK), TOK)
            code = codes_ref[where, :].astype(f32)
            want = wanted(row, side, lax.convert_element_type(b, f32))
            hit = jnp.zeros((TOK, NX * rows), f32)
            for k in range(TOP):
                hit = jnp.where(want == code[:, k : k + 1], 1.0, hit)
            out[pl.ds(pl.multiple_of(b * TOK, TOK), TOK), :] = hit.astype(bf16)
            return 0

        lax.fori_loop(0, blocks, block, 0)

    return pl.pallas_call(
        kernel,
        out_shape=pltpu.VMEM((blocks * TOK, NX * rows), bf16),
        in_specs=[VMEM_SPEC],
        out_specs=VMEM_SPEC,
        compiler_params=params(),
        name="hots",
    )(codes)


def combine(hot, rows_in, slots, adds, last=False, split=1):
    nb = len(slots)
    added = [a for p in adds for a, _ in p]
    na = len(added)

    def kernel(hot_ref, *refs):
        src, extra, outs = refs[:NX], refs[NX : NX + na], refs[NX + na :]

        def column(i, _):
            where = pl.ds(pl.multiple_of(i * TILE, TILE), TILE)
            data = stacked([s[:, where] for s in src])
            at = 0
            for b in range(nb):
                mine = jnp.dot(
                    hot_ref[slots[b] * TOK : (slots[b] + 1) * TOK, :],
                    data,
                    preferred_element_type=f32,
                )
                for _, (first, count) in adds[b]:
                    more = extra[at][:, where].astype(f32)
                    at += 1
                    if count < TOK:
                        pad = jnp.zeros((TOK - count, TILE), f32)
                        more = jnp.concatenate(
                            [more, pad] if first == 0 else [pad, more], axis=0
                        )
                    mine = mine + more
                mine = mine.astype(bf16)
                part = TOK // split
                for h in range(split):
                    outs[b * split + h][:, where] = mine[h * part : (h + 1) * part]
            return 0

        lax.fori_loop(0, D // TILE, column, 0)

    kind = (lambda s, t: jax.ShapeDtypeStruct(s, t)) if last else pltpu.VMEM
    return pl.pallas_call(
        kernel,
        out_shape=[kind((TOK // split, D), bf16)] * (nb * split),
        in_specs=[VMEM_SPEC] * (1 + NX + na),
        out_specs=[VMEM_SPEC] * (nb * split),
        compiler_params=params(),
        name="combine",
    )(*near([hot, *rows_in, *added]))


def order_kernel(me_ref, loss_ref, up_ref, out, loss_out):
    loss_out[...] = jnp.full((8, FF), loss_ref[0], f32)
    x, z = me_ref[0], me_ref[1]
    picks = []
    for c, offsets in enumerate(CHUNKS):
        rows = ROWS[c]
        row = lax.broadcasted_iota(jnp.int32, (rows, NZ * CAP), 0)
        col = lax.broadcasted_iota(jnp.int32, (rows, NZ * CAP), 1)
        want = jnp.full((rows, NZ * CAP), -1, jnp.int32)
        for b, offset in enumerate(offsets):
            block = lax.rem(z + offset + NZ, NZ)
            inside = (row >= CAP * b) & (row < CAP * (b + 1))
            want = jnp.where(inside, block * CAP + row - CAP * b, want)
        picks.append(jnp.where(want == col, 1.0, 0.0).astype(bf16))

    def columns(i, _):
        where = pl.ds(pl.multiple_of(i * 256, 128), 256)
        got = []
        for pick in picks:
            for dx in range(NX):
                source = lax.rem(x - dx + NX, NX)
                start = pl.multiple_of(source * (NZ * CAP), 16)
                part = up_ref[pl.ds(start, NZ * CAP), where]
                got.append(jnp.dot(pick, part, preferred_element_type=f32))
        out[:, where] = jnp.concatenate(got, axis=0).astype(bf16)
        return 0

    lax.fori_loop(0, FF // 256, columns, 0)


def ordered(me, loss, up):
    return pl.pallas_call(
        order_kernel,
        out_shape=[
            jax.ShapeDtypeStruct((ALL_ROWS, FF), bf16),
            jax.ShapeDtypeStruct((8, FF), f32),
        ],
        in_specs=[SMEM_SPEC, SMEM_SPEC, VMEM_SPEC],
        out_specs=[VMEM_SPEC] * 2,
        compiler_params=params(),
        name="order",
    )(me, loss.reshape(1), up)


def slot_grads(me, ups, same, other):
    order = sorted(BACK)
    flat = [(p, dx) for p in order for dx in range(NX)]
    step = 256

    def kernel(me_ref, up, mine, theirs, *refs):
        outs, w = refs[:-1], refs[-1]
        first = me_ref[3] == 0

        def chip(i, _):
            a, b = mine[i], theirs[i]
            w[pl.ds(pl.multiple_of(i * 2 * SHARD, SHARD), SHARD), :] = jnp.where(first, a, b)
            w[pl.ds(pl.multiple_of(i * 2 * SHARD + SHARD, SHARD), SHARD), :] = jnp.where(
                first, b, a
            )
            return 0

        lax.fori_loop(0, NY, chip, 0)

        def column(i, _):
            where = pl.ds(pl.multiple_of(i * step, step), step)
            got = lax.dot_general(
                up[...], w[where, :], (((1,), (1,)), ((), ())), preferred_element_type=f32
            )
            for out, (p, dx) in zip(outs, flat):
                c, _, _, start, rows = BACK[p]
                at = STARTS[c] + dx * ROWS[c] + start
                out[:, where] = got[at : at + rows].astype(bf16)
            return 0

        lax.fori_loop(0, D // step, column, 0)

    out = pl.pallas_call(
        kernel,
        out_shape=[pltpu.VMEM((BACK[p][4], D), bf16) for p, _ in flat],
        in_specs=[SMEM_SPEC] + [VMEM_SPEC] * 3,
        out_specs=[VMEM_SPEC] * len(flat),
        scratch_shapes=[pltpu.VMEM((D, FF), bf16)],
        compiler_params=params(mib=12),
        name="slot_grads",
    )(me, *near([ups, same, other]))
    return {p: out[i * NX : (i + 1) * NX] for i, p in enumerate(order)}


def products(src, up, where):
    slab = stacked([s[:, where] for s in src])
    return lax.dot_general(slab, up, (((0,), (0,)), ((), ())), preferred_element_type=f32)


def partial_of(rows_in, ups, error):
    flat = [a for c in rows_in for a in c]
    used = sum(a.shape[0] for a in flat)
    wide = 2 * SHARD

    def kernel(up, err, *refs):
        src, out = refs[:-1], refs[-1]

        def tile(i, _):
            where = pl.ds(pl.multiple_of(i * wide, 128), wide)
            out[where, :] = err[where, :].astype(f32) + products(src, up[:used, :], where)
            return 0

        lax.fori_loop(0, NY, tile, 0)

    return pl.pallas_call(
        kernel,
        out_shape=pltpu.VMEM((D, FF), f32),
        in_specs=[VMEM_SPEC] * (2 + len(flat)),
        out_specs=VMEM_SPEC,
        compiler_params=params(mib=12),
        name="partial",
    )(*near([ups, error, *flat]))


def levels_of(me, rows_in, ups, total):
    start = ALL_ROWS - sum(a.shape[0] for a in rows_in)
    wide = 2 * SHARD

    def kernel(me_ref, up, tot, *refs):
        src, (keep, give) = refs[:NX], refs[NX:]
        first = me_ref[3] == 0

        def tile(i, _):
            where = pl.ds(pl.multiple_of(i * wide, 128), wide)
            total = tot[where, :] + products(src, up[start:, :], where)
            lane = lax.broadcasted_iota(jnp.int32, (wide, QB), 1)
            scales = jnp.zeros((wide, QB), f32)

            def store(value, columns):
                a, b = value[:SHARD].astype(bf16), value[SHARD:].astype(bf16)
                keep[i, :, columns] = jnp.where(first, a, b)
                give[i, :, columns] = jnp.where(first, b, a)

            for q in range(NQ):
                block = total[:, q * QB : (q + 1) * QB]
                top = jnp.max(jnp.abs(block), axis=1, keepdims=True)
                scale = ((top + amax_eps) / quant_top).astype(bf16).astype(f32)
                store(block * (1.0 / scale), slice(q * QB, (q + 1) * QB))
                scales = jnp.where(lane == q, scale, scales)
            store(scales, slice(FF, WIDE))
            return 0

        lax.fori_loop(0, NY, tile, 0)

    return pl.pallas_call(
        kernel,
        out_shape=[pltpu.VMEM((NY, SHARD, WIDE), bf16)] * 2,
        in_specs=[SMEM_SPEC] + [VMEM_SPEC] * (2 + NX),
        out_specs=[VMEM_SPEC] * 2,
        compiler_params=params(mib=12),
        name="levels",
    )(me, *near([ups, total, *rows_in]))


def pair_sums(me, kept, given):
    def kernel(me_ref, a_ref, b_ref, *outs):
        y = me_ref[2]
        spread = (
            lax.broadcasted_iota(jnp.int32, (QB, FF), 0)
            == lax.broadcasted_iota(jnp.int32, (QB, FF), 1) // QB
        )
        spread = jnp.where(spread, 1.0, 0.0).astype(bf16)
        for k in range(NY):
            chip = lax.rem(y + k, NY)
            total = jnp.zeros((SHARD, FF), f32)
            for ref in (a_ref, b_ref):
                scale = jnp.dot(ref[chip, :, FF:], spread, preferred_element_type=f32)
                total = total + ref[chip, :, :FF].astype(f32) * scale
            outs[k][...] = total.astype(bf16)

    return pl.pallas_call(
        kernel,
        out_shape=[pltpu.VMEM((SHARD, FF), bf16)] * NY,
        in_specs=[SMEM_SPEC] + [VMEM_SPEC] * 2,
        out_specs=[VMEM_SPEC] * NY,
        compiler_params=params(mib=8),
        name="pair_sums",
    )(me, *near([kept, given]))


def adam(loss, sums, w, m, v):
    part = 32

    def kernel(loss_ref, *refs):
        got, (w_ref, m_ref, v_ref, nw_ref, nm_ref, nv_ref) = refs[:NY], refs[NY:]

        def rows(i, _):
            where = pl.ds(pl.multiple_of(i * part, part), part)
            total = got[0][where, :].astype(f32)
            for g in got[1:]:
                total = total + g[where, :].astype(f32)
            gradient = total / loss_ref[0:1, :]
            first = beta_one * m_ref[where, :].astype(f32) + (1.0 - beta_one) * gradient
            second = (
                beta_two * v_ref[where, :].astype(f32) + (1.0 - beta_two) * gradient * gradient
            )
            first_hat = first / (1.0 - beta_one**STEP)
            second_hat = second / (1.0 - beta_two**STEP)
            master = w_ref[where, :].astype(f32)
            updated = master - learn_rate * (
                first_hat / (jnp.sqrt(second_hat) + adam_eps) + decay_rate * master
            )
            nw_ref[where, :] = updated.astype(bf16)
            nm_ref[where, :] = first.astype(bf16)
            nv_ref[where, :] = second.astype(bf16)
            return 0

        lax.fori_loop(0, SHARD // part, rows, 0)

    return pl.pallas_call(
        kernel,
        out_shape=[pltpu.VMEM((SHARD, FF), bf16)]
        + [jax.ShapeDtypeStruct((SHARD, FF), bf16)] * 2,
        in_specs=[VMEM_SPEC] * (NY + 4),
        out_specs=[VMEM_SPEC] * 3,
        compiler_params=params(mib=8),
        name="adam",
    )(loss, *near(sums), *far([w, m, v]))


def place_shards(me, shards):
    def kernel(me_ref, *refs):
        parts, out, side, sems = refs[:NY], refs[NY], refs[NY + 1], refs[NY + 2]
        y, core = me_ref[2], me_ref[3]
        copies = []
        for k, part in enumerate(parts):
            place = lax.rem(y - k + NY, NY) * 2 + core
            rows = pl.ds(pl.multiple_of(place * SHARD, SHARD), SHARD)
            copies.append(pltpu.make_async_copy(part, side.at[k], sems.at[k]))
            copies.append(pltpu.make_async_copy(part, out.at[0, rows, :], sems.at[NY + k]))
        for copy in copies:
            copy.start()
        for copy in copies:
            copy.wait()

    return pl.pallas_call(
        kernel,
        out_shape=[pltpu.HBM((1, D, FF), bf16), pltpu.VMEM((NY, SHARD, FF), bf16)],
        in_specs=[SMEM_SPEC] + [pl.BlockSpec(memory_space=pl.ANY)] * NY,
        out_specs=[pl.BlockSpec(memory_space=pl.ANY)] * 2,
        scratch_shapes=[pltpu.SemaphoreType.DMA((2 * NY,))],
        compiler_params=params(mib=2),
        name="place",
    )(me, *shards)


def assemble(me, full, other):
    def kernel(me_ref, _, side, out, sems):
        y, core = me_ref[2], me_ref[3]
        copies = []
        for k in range(NY):
            place = lax.rem(y - k + NY, NY) * 2 + 1 - core
            rows = pl.ds(pl.multiple_of(place * SHARD, SHARD), SHARD)
            copies.append(pltpu.make_async_copy(side.at[k], out.at[0, rows, :], sems.at[k]))
        for copy in copies:
            copy.start()
        for copy in copies:
            copy.wait()

    return pl.pallas_call(
        kernel,
        out_shape=pltpu.HBM((1, D, FF), bf16),
        in_specs=[SMEM_SPEC] + [pl.BlockSpec(memory_space=pl.ANY)] * 2,
        out_specs=pl.BlockSpec(memory_space=pl.ANY),
        scratch_shapes=[pltpu.SemaphoreType.DMA((NY,))],
        input_output_aliases={1: 0},
        compiler_params=params(mib=2),
        name="assemble",
    )(me, full, other)


def step(tokens, routing, grad_up, up_shard, error_feedback, moment_one, moment_two, loss):
    def send(a, axis, n, shift):
        pairs = [(i, (i + shift) % n) for i in range(n)]
        return lax.ppermute(a, axis, pairs)

    def send_x(arrays, sign):
        return [arrays[0]] + [send(arrays[dx], "x", NX, sign * dx) for dx in range(1, NX)]

    def send_z(a, b):
        return send(a, "z", NZ, 1), send(b, "z", NZ, -1)

    def send_y(arrays):
        return [arrays[0]] + [send(arrays[k], "y", NY, k) for k in range(1, NY)]

    def swap(a):
        return lax.ppermute(a, "core", [(0, 1), (1, 0)])

    me = jnp.stack([lax.axis_index(a) for a in ("x", "z", "y", "core")]).astype(jnp.int32)
    same = jnp.broadcast_to(up_shard, (NY, SHARD, FF))
    same = lax.all_to_all(same, "y", split_axis=0, concat_axis=0, tiled=True)
    other = swap(same)

    half = TOK // 2
    ext = prep(jnp.transpose(routing), tokens)
    block = {0: [ext]}
    up, down = ext, ext
    for r in (1, 2, 3):
        up, down = send_z(up, down)
        block[-r], block[r] = [up], [down]
    block[4] = list(send_z(up[:half], down[half:]))

    arrived, codes = [], []
    for offsets, rows in zip(CHUNKS, ROWS):
        out, code = dispatch(me, [block[o] for o in offsets], rows)
        arrived.append(send_x(out, 1))
        codes.append(code)
    hot = {p: hots(codes[BACK[p][0]], p) for p in BACK}

    ups, loss_row = ordered(me, loss, grad_up[0])
    returned = slot_grads(me, ups, same, other)
    total = partial_of(arrived[:2], ups, error_feedback[0])
    kept, given = levels_of(me, arrived[2], ups, total)
    sums = pair_sums(me, kept, swap(given))
    sums = send_y(sums)
    new_w, new_m, new_v = adam(loss_row, sums, up_shard[0], moment_one[0], moment_two[0])
    full, side = place_shards(me, send_y([new_w] * NY))
    full = assemble(me, full, swap(side))

    back = {p: send_x(returned[p], -1) for p in (4, 3, 2, 0)}
    top, low, whole = (0, half), (half, half), (0, TOK)
    u, d = combine(hot[4], back[4], [0], [[]], split=2)
    u, d = send_z(u, d)
    u, d = combine(hot[3], back[3], [1, 0], [[(u, top)], [(d, low)]])
    u, d = send_z(u, d)
    u, d = combine(hot[2], back[2], [1, 0], [[(u, whole)], [(d, whole)]])
    u, d = send_z(u, d)
    u, d = combine(hot[0], back[0], [2, 1], [[(u, whole)], [(d, whole)]])
    u, d = send_z(u, d)
    (grad_tokens,) = combine(hot[0], back[0], [0], [[(u, whole), (d, whole)]], last=True)
    return (grad_tokens, full, new_m[None], new_v[None])


def solution(mesh):
    fine = Mesh(mesh.devices.reshape(NX, NZ, NY, 2), ("x", "z", "y", "core"))
    expert = ("x", "z")
    in_specs = (
        P(("x", "z", "y", "core"), None),
        P(("x", "z", "y", "core"), None),
        P(expert, ("y", "core"), None),
        P(expert, ("y", "core"), None),
        P(expert, ("y", "core"), None),
        P(expert, ("y", "core"), None),
        P(expert, ("y", "core"), None),
        P(),
    )
    out_specs = (
        P(("x", "z", "y", "core"), None),
        P(expert, None, None),
        P(expert, ("y", "core"), None),
        P(expert, ("y", "core"), None),
    )
    return jax.shard_map(step, mesh=fine, in_specs=in_specs, out_specs=out_specs, check_vma=False)
```

```python
import jax
import jax.numpy as jnp
from jax import lax
from jax.experimental import pallas as pl
from jax.experimental.pallas import tpu as pltpu
from jax.sharding import Mesh, PartitionSpec as P

D = 2560
FF = 768
TOP = 6
QB = 128
NQ = FF // QB
STEP = 20
TOK = 128
CAP = 36
NX = 4
NZ = 8
NDP = 8
NY = 4
SHARD = D // NDP
INFO = 128
EXT = D + INFO
WIDE = FF + 128

learn_rate = 0.001
beta_one = 0.9
beta_two = 0.999
decay_rate = 0.1
adam_eps = 1e-08
quant_top = 127.0
amax_eps = 1e-06

CHUNKS = ((0, -1, 1), (-2, 2), (-3, 3, 4))
ROWS = tuple(-(-len(c) * CAP // 8) * 8 for c in CHUNKS)
BACK = {0: (0, 0, 3, 0, 112), 2: (1, 0, 2, 0, 72), 3: (2, 0, 2, 0, 72), 4: (2, 2, 1, 72, 40)}
bf16 = jnp.bfloat16
f32 = jnp.float32


VMEM = pltpu.MemorySpace.VMEM
SMEM_SPEC = pl.BlockSpec(memory_space=pltpu.MemorySpace.SMEM)
VMEM_SPEC = pl.BlockSpec(memory_space=VMEM)
STARTS = tuple(NX * sum(ROWS[:c]) for c in range(len(ROWS)))
ALL_ROWS = NX * sum(ROWS)


def params(n=0, mib=6):
    if n == 0:
        return pltpu.CompilerParams(vmem_limit_bytes=mib << 20)
    return pltpu.CompilerParams(
        dimension_semantics=("arbitrary",) * n, vmem_limit_bytes=mib << 20
    )


def near(arrays):
    return [pltpu.with_memory_space_constraint(a, VMEM) for a in arrays]


def far(arrays):
    return [pltpu.with_memory_space_constraint(a, pltpu.MemorySpace.HBM) for a in arrays]


def prep_kernel(routing_ref, tokens_ref, ext_ref):
    r = routing_ref[...]
    down = lax.broadcasted_iota(jnp.int32, (INFO, TOK), 0)
    across = lax.broadcasted_iota(jnp.int32, (INFO, TOK), 1)
    named = jnp.zeros((INFO, TOK), f32)
    for k in range(TOP):
        named = named + jnp.where(r[k : k + 1, :] == down, 1.0, 0.0)
    earlier = jnp.where(down < across, 1.0, 0.0).astype(bf16)
    before = jnp.dot(named.astype(bf16), earlier, preferred_element_type=f32)
    info = jnp.zeros((INFO, TOK), f32)
    for k in range(TOP):
        e = r[k : k + 1, :]
        w = jnp.sum(jnp.where(e == down, before, 0.0), axis=0, keepdims=True)
        info = jnp.where(down == k, e.astype(f32), info)
        info = jnp.where(down == TOP + k, w, info)
    ext_ref[:, :D] = tokens_ref[...]
    ext_ref[:, D:] = jnp.transpose(info).astype(bf16)


def prep(routing, tokens):
    return pl.pallas_call(
        prep_kernel,
        out_shape=pltpu.VMEM((TOK, EXT), bf16),
        in_specs=[VMEM_SPEC] * 2,
        out_specs=VMEM_SPEC,
        compiler_params=params(),
        name="prep",
    )(routing, tokens)


def stacked(parts):
    if all(p.shape[0] % 16 == 0 for p in parts):
        return jnp.concatenate(parts, axis=0)
    return jnp.concatenate([p.astype(f32) for p in parts], axis=0).astype(bf16)


def joined(parts):
    return parts[0] if len(parts) == 1 else jnp.concatenate(parts, axis=0)


def slot_of(e, w, x, z):
    ex = jnp.floor(e * 0.125)
    ez = e - ex * 8.0
    dx = ex - x
    dx = jnp.where(dx < 0.0, dx + float(NX), dx)
    return jnp.where(ez == z, dx * 64.0 + w, -1.0)


def placed(at, rows):
    side = jnp.floor((at + 0.5) * (1.0 / rows))
    return at - side * float(rows), side


def wanted(row, side, b):
    at = row - b * float(CAP)
    return jnp.where((at >= 0.0) & (at < float(CAP)), at + 64.0 * side, -2.0)


def dispatch(me, blocks, rows):
    nb = len(blocks)
    flat = [a for b in blocks for a in b]
    sizes = [len(b) for b in blocks]
    nf = len(flat)
    high = -(-rows // 16) * 16

    def kernel(me_ref, *refs):
        tok, outs = refs[:nf], refs[nf : nf + NX]
        codes, hot, code = refs[nf + NX :]
        x = me_ref[0].astype(f32)
        z = me_ref[1].astype(f32)
        row = lax.broadcasted_iota(jnp.int32, (high, TOK), 0).astype(f32)
        at = 0
        for b in range(nb):
            raw = joined([t[:, D:] for t in tok[at : at + sizes[b]]]).astype(f32)
            at += sizes[b]
            codes[b * TOK : (b + 1) * TOK, :] = slot_of(
                raw, pltpu.roll(raw, INFO - TOP, 1), x, z
            ).astype(bf16)
            info = jnp.transpose(raw)
            code[8 * b : 8 * b + TOP, :] = slot_of(info[0:TOP], info[TOP : 2 * TOP], x, z)

        def side(dx, _):
            for b in range(nb):
                want = wanted(row, lax.convert_element_type(dx, f32), b)
                hit = jnp.zeros((high, TOK), f32)
                for k in range(TOP):
                    hit = jnp.where(want == code[8 * b + k : 8 * b + k + 1, :], 1.0, hit)
                where = pl.ds(pl.multiple_of(dx * high, 16), high)
                hot[where, b * TOK : (b + 1) * TOK] = hit.astype(bf16)
            return 0

        lax.fori_loop(0, NX, side, 0)

        def column(i, _):
            where = pl.ds(pl.multiple_of(i * 256, 256), 256)
            t = joined([t[:, where] for t in tok])
            got = jnp.dot(hot[...], t, preferred_element_type=f32)
            for dx in range(NX):
                outs[dx][:, where] = got[dx * high : dx * high + rows].astype(bf16)
            return 0

        lax.fori_loop(0, D // 256, column, 0)

    out = pl.pallas_call(
        kernel,
        out_shape=[pltpu.VMEM((rows, D), bf16)] * NX
        + [jax.ShapeDtypeStruct((nb * TOK, INFO), bf16)],
        in_specs=[SMEM_SPEC] + [VMEM_SPEC] * nf,
        out_specs=[VMEM_SPEC] * (NX + 1),
        scratch_shapes=[pltpu.VMEM((NX * high, nb * TOK), bf16), pltpu.VMEM((8 * nb, TOK), f32)],
        compiler_params=params(),
        name="dispatch",
    )(me, *near(flat))
    return out[:NX], out[NX]


def hots(codes, piece):
    _, start, blocks, _, rows = BACK[piece]

    def kernel(codes_ref, out):
        lane = lax.broadcasted_iota(jnp.int32, (TOK, NX * rows), 1).astype(f32)
        row, side = placed(lane, rows)

        def block(b, _):
            where = pl.ds(pl.multiple_of((start + b) * TOK, TOK), TOK)
            code = codes_ref[where, :].astype(f32)
            want = wanted(row, side, lax.convert_element_type(b, f32))
            hit = jnp.zeros((TOK, NX * rows), f32)
            for k in range(TOP):
                hit = jnp.where(want == code[:, k : k + 1], 1.0, hit)
            out[pl.ds(pl.multiple_of(b * TOK, TOK), TOK), :] = hit.astype(bf16)
            return 0

        lax.fori_loop(0, blocks, block, 0)

    return pl.pallas_call(
        kernel,
        out_shape=pltpu.VMEM((blocks * TOK, NX * rows), bf16),
        in_specs=[VMEM_SPEC],
        out_specs=VMEM_SPEC,
        compiler_params=params(),
        name="hots",
    )(codes)


def combine(hot, rows_in, slots, adds, last=False, split=1):
    nb = len(slots)
    added = [a for p in adds for a, _ in p]
    na = len(added)

    def kernel(hot_ref, *refs):
        src, extra, outs = refs[:NX], refs[NX : NX + na], refs[NX + na :]

        def column(i, _):
            where = pl.ds(pl.multiple_of(i * 256, 256), 256)
            data = stacked([s[:, where] for s in src])
            at = 0
            for b in range(nb):
                mine = jnp.dot(
                    hot_ref[slots[b] * TOK : (slots[b] + 1) * TOK, :],
                    data,
                    preferred_element_type=f32,
                )
                for _, (first, count) in adds[b]:
                    more = extra[at][:, where].astype(f32)
                    at += 1
                    if count < TOK:
                        pad = jnp.zeros((TOK - count, 256), f32)
                        more = jnp.concatenate(
                            [more, pad] if first == 0 else [pad, more], axis=0
                        )
                    mine = mine + more
                mine = mine.astype(bf16)
                part = TOK // split
                for h in range(split):
                    outs[b * split + h][:, where] = mine[h * part : (h + 1) * part]
            return 0

        lax.fori_loop(0, D // 256, column, 0)

    kind = (lambda s, t: jax.ShapeDtypeStruct(s, t)) if last else pltpu.VMEM
    return pl.pallas_call(
        kernel,
        out_shape=[kind((TOK // split, D), bf16)] * (nb * split),
        in_specs=[VMEM_SPEC] * (1 + NX + na),
        out_specs=[VMEM_SPEC] * (nb * split),
        compiler_params=params(),
        name="combine",
    )(*near([hot, *rows_in, *added]))


def order_kernel(me_ref, loss_ref, up_ref, out, loss_out, rows):
    loss_out[...] = jnp.full((8, FF), loss_ref[0], f32)
    x, z = me_ref[0], me_ref[1]
    picks = []
    for c, offsets in enumerate(CHUNKS):
        row = lax.broadcasted_iota(jnp.int32, (ROWS[c], NZ * CAP), 0)
        col = lax.broadcasted_iota(jnp.int32, (ROWS[c], NZ * CAP), 1)
        want = jnp.full((ROWS[c], NZ * CAP), -1, jnp.int32)
        for b, offset in enumerate(offsets):
            block = lax.rem(z + offset + NZ, NZ)
            inside = (row >= CAP * b) & (row < CAP * (b + 1))
            want = jnp.where(inside, block * CAP + row - CAP * b, want)
        picks.append(jnp.where(want == col, 1.0, 0.0).astype(bf16))

    def side(dx, _):
        source = lax.rem(x - dx + NX, NX)
        start = pl.multiple_of(source * (NZ * CAP), 16)
        part = up_ref[pl.ds(start, NZ * CAP), :]
        for c, pick in enumerate(picks):
            at = pl.multiple_of(STARTS[c] + dx * ROWS[c], 8)
            rows[pl.ds(at, ROWS[c]), :] = jnp.dot(pick, part, preferred_element_type=f32)
        return 0

    lax.fori_loop(0, NX, side, 0)
    high = 32

    def narrow(i, _):
        where = pl.ds(pl.multiple_of(i * high, high), high)
        out[where, :] = rows[where, :].astype(bf16)
        return 0

    lax.fori_loop(0, ALL_ROWS // high, narrow, 0)


def ordered(me, loss, up):
    return pl.pallas_call(
        order_kernel,
        out_shape=[
            jax.ShapeDtypeStruct((ALL_ROWS, FF), bf16),
            jax.ShapeDtypeStruct((8, FF), f32),
        ],
        in_specs=[SMEM_SPEC, SMEM_SPEC, VMEM_SPEC],
        out_specs=[VMEM_SPEC] * 2,
        scratch_shapes=[pltpu.VMEM((ALL_ROWS, FF), f32)],
        compiler_params=params(mib=10),
        name="order",
    )(me, loss.reshape(1), up)


def slot_grads(me, ups, same, other):
    order = sorted(BACK)
    flat = [(p, dx) for p in order for dx in range(NX)]
    step = 256

    def kernel(me_ref, up, mine, theirs, *refs):
        outs, w = refs[:-1], refs[-1]
        first = me_ref[3] == 0

        def chip(i, _):
            a, b = mine[i], theirs[i]
            w[pl.ds(pl.multiple_of(i * 2 * SHARD, SHARD), SHARD), :] = jnp.where(first, a, b)
            w[pl.ds(pl.multiple_of(i * 2 * SHARD + SHARD, SHARD), SHARD), :] = jnp.where(
                first, b, a
            )
            return 0

        lax.fori_loop(0, NY, chip, 0)

        def column(i, _):
            where = pl.ds(pl.multiple_of(i * step, step), step)
            got = lax.dot_general(
                up[...], w[where, :], (((1,), (1,)), ((), ())), preferred_element_type=f32
            )
            for out, (p, dx) in zip(outs, flat):
                c, _, _, start, rows = BACK[p]
                at = STARTS[c] + dx * ROWS[c] + start
                out[:, where] = got[at : at + rows].astype(bf16)
            return 0

        lax.fori_loop(0, D // step, column, 0)

    out = pl.pallas_call(
        kernel,
        out_shape=[pltpu.VMEM((BACK[p][4], D), bf16) for p, _ in flat],
        in_specs=[SMEM_SPEC] + [VMEM_SPEC] * 3,
        out_specs=[VMEM_SPEC] * len(flat),
        scratch_shapes=[pltpu.VMEM((D, FF), bf16)],
        compiler_params=params(mib=12),
        name="slot_grads",
    )(me, *near([ups, same, other]))
    return {p: out[i * NX : (i + 1) * NX] for i, p in enumerate(order)}


def products(src, up, where):
    slab = stacked([s[:, where] for s in src])
    return lax.dot_general(slab, up, (((0,), (0,)), ((), ())), preferred_element_type=f32)


def partial_of(rows_in, ups, error):
    flat = [a for c in rows_in for a in c]
    used = sum(a.shape[0] for a in flat)
    wide = 256

    def kernel(up, err, *refs):
        src, out = refs[:-1], refs[-1]

        def tile(i, _):
            where = pl.ds(pl.multiple_of(i * wide, 128), wide)
            out[where, :] = err[where, :].astype(f32) + products(src, up[:used, :], where)
            return 0

        lax.fori_loop(0, D // wide, tile, 0)

    return pl.pallas_call(
        kernel,
        out_shape=pltpu.VMEM((D, FF), f32),
        in_specs=[VMEM_SPEC] * (2 + len(flat)),
        out_specs=VMEM_SPEC,
        compiler_params=params(mib=12),
        name="partial",
    )(*near([ups, error, *flat]))


def levels_of(me, rows_in, ups, total):
    start = ALL_ROWS - sum(a.shape[0] for a in rows_in)
    wide = 2 * SHARD

    def kernel(me_ref, up, tot, *refs):
        src, (keep, give) = refs[:NX], refs[NX:]
        first = me_ref[3] == 0

        def tile(i, _):
            where = pl.ds(pl.multiple_of(i * wide, 128), wide)
            total = tot[where, :] + products(src, up[start:, :], where)
            lane = lax.broadcasted_iota(jnp.int32, (wide, QB), 1)
            scales = jnp.zeros((wide, QB), f32)

            def store(value, columns):
                a, b = value[:SHARD].astype(bf16), value[SHARD:].astype(bf16)
                keep[i, :, columns] = jnp.where(first, a, b)
                give[i, :, columns] = jnp.where(first, b, a)

            for q in range(NQ):
                block = total[:, q * QB : (q + 1) * QB]
                top = jnp.max(jnp.abs(block), axis=1, keepdims=True)
                scale = ((top + amax_eps) / quant_top).astype(bf16).astype(f32)
                store(block * (1.0 / scale), slice(q * QB, (q + 1) * QB))
                scales = jnp.where(lane == q, scale, scales)
            store(scales, slice(FF, WIDE))
            return 0

        lax.fori_loop(0, NY, tile, 0)

    return pl.pallas_call(
        kernel,
        out_shape=[pltpu.VMEM((NY, SHARD, WIDE), bf16)] * 2,
        in_specs=[SMEM_SPEC] + [VMEM_SPEC] * (2 + NX),
        out_specs=[VMEM_SPEC] * 2,
        compiler_params=params(mib=12),
        name="levels",
    )(me, *near([ups, total, *rows_in]))


def pair_sums(kept, given):
    part = 64

    def kernel(a_ref, b_ref, out, total, sems):
        spread = (
            lax.broadcasted_iota(jnp.int32, (QB, FF), 0)
            == lax.broadcasted_iota(jnp.int32, (QB, FF), 1) // QB
        )
        spread = jnp.where(spread, 1.0, 0.0).astype(bf16)

        def copy(i):
            return pltpu.make_async_copy(total.at[i], out.at[i], sems.at[i])

        def chip(i, _):
            def rows(j, _):
                where = pl.ds(pl.multiple_of(j * part, part), part)
                both = jnp.zeros((part, FF), f32)
                for ref in (a_ref, b_ref):
                    scale = jnp.dot(ref[i, where, FF:], spread, preferred_element_type=f32)
                    both = both + ref[i, where, :FF].astype(f32) * scale
                total[i, where, :] = both.astype(bf16)
                return 0

            lax.fori_loop(0, SHARD // part, rows, 0)
            copy(i).start()
            return 0

        lax.fori_loop(0, NY, chip, 0)
        for i in range(NY):
            copy(i).wait()

    return pl.pallas_call(
        kernel,
        out_shape=pltpu.HBM((NY, SHARD, FF), bf16),
        in_specs=[VMEM_SPEC] * 2,
        out_specs=pl.BlockSpec(memory_space=pl.ANY),
        scratch_shapes=[pltpu.VMEM((NY, SHARD, FF), bf16), pltpu.SemaphoreType.DMA((NY,))],
        compiler_params=params(mib=8),
        name="pair_sums",
    )(*near([kept, given]))


def adam(loss, sums, w, m, v):
    part = 32

    def kernel(loss_ref, *refs):
        got, w_ref, m_ref, v_ref, nw_ref, nm_ref, nv_ref = refs

        def rows(i, _):
            where = pl.ds(pl.multiple_of(i * part, part), part)
            total = got[0, where, :].astype(f32)
            for k in range(1, NY):
                total = total + got[k, where, :].astype(f32)
            gradient = total / loss_ref[0:1, :]
            first = beta_one * m_ref[where, :].astype(f32) + (1.0 - beta_one) * gradient
            second = (
                beta_two * v_ref[where, :].astype(f32) + (1.0 - beta_two) * gradient * gradient
            )
            first_hat = first / (1.0 - beta_one**STEP)
            second_hat = second / (1.0 - beta_two**STEP)
            master = w_ref[where, :].astype(f32)
            updated = master - learn_rate * (
                first_hat / (jnp.sqrt(second_hat) + adam_eps) + decay_rate * master
            )
            for k in range(NY):
                nw_ref[k, where, :] = updated.astype(bf16)
            nm_ref[where, :] = first.astype(bf16)
            nv_ref[where, :] = second.astype(bf16)
            return 0

        lax.fori_loop(0, SHARD // part, rows, 0)

    return pl.pallas_call(
        kernel,
        out_shape=[pltpu.HBM((NY, SHARD, FF), bf16)]
        + [jax.ShapeDtypeStruct((SHARD, FF), bf16)] * 2,
        in_specs=[VMEM_SPEC] * 5,
        out_specs=[VMEM_SPEC] * 3,
        compiler_params=params(mib=8),
        name="adam",
    )(loss, *far([sums, w, m, v]))


def assemble(me, same, other):
    def kernel(me_ref, a_ref, b_ref, out, sems):
        core = me_ref[3]
        copies = []
        for i in range(2 * NY):
            shards, owner = (a_ref, core) if i < NY else (b_ref, 1 - core)
            place = (i % NY) * 2 + owner
            rows = pl.ds(pl.multiple_of(place * SHARD, SHARD), SHARD)
            copies.append(
                pltpu.make_async_copy(shards.at[i % NY], out.at[0, rows, :], sems.at[i])
            )
        for copy in copies:
            copy.start()
        for copy in copies:
            copy.wait()

    return pl.pallas_call(
        kernel,
        out_shape=pltpu.HBM((1, D, FF), bf16),
        in_specs=[SMEM_SPEC] + [pl.BlockSpec(memory_space=pl.ANY)] * 2,
        out_specs=pl.BlockSpec(memory_space=pl.ANY),
        scratch_shapes=[pltpu.SemaphoreType.DMA((2 * NY,))],
        compiler_params=params(mib=2),
        name="assemble",
    )(me, same, other)


def step(tokens, routing, grad_up, up_shard, error_feedback, moment_one, moment_two, loss):
    def send(a, axis, n, shift):
        pairs = [(i, (i + shift) % n) for i in range(n)]
        return lax.ppermute(a, axis, pairs)

    def send_x(arrays, sign):
        return [arrays[0]] + [send(arrays[dx], "x", NX, sign * dx) for dx in range(1, NX)]

    def send_z(a, b):
        return send(a, "z", NZ, 1), send(b, "z", NZ, -1)

    def send_y(a):
        return lax.all_to_all(a, "y", split_axis=0, concat_axis=0, tiled=True)

    def swap(a):
        return lax.ppermute(a, "core", [(0, 1), (1, 0)])

    me = jnp.stack([lax.axis_index(a) for a in ("x", "z", "y", "core")]).astype(jnp.int32)
    same = send_y(jnp.broadcast_to(up_shard, (NY, SHARD, FF)))
    other = swap(same)

    half = TOK // 2
    ext = prep(jnp.transpose(routing), tokens)
    block = {0: [ext]}
    up, down = ext, ext
    for r in (1, 2, 3):
        up, down = send_z(up, down)
        block[-r], block[r] = [up], [down]
    block[4] = list(send_z(up[:half], down[half:]))

    arrived, codes = [], []
    for offsets, rows in zip(CHUNKS, ROWS):
        out, code = dispatch(me, [block[o] for o in offsets], rows)
        arrived.append(send_x(out, 1))
        codes.append(code)
    hot = {p: hots(codes[BACK[p][0]], p) for p in BACK}

    ups, loss_row = ordered(me, loss, grad_up[0])
    returned = slot_grads(me, ups, same, other)
    total = partial_of(arrived[:2], ups, error_feedback[0])
    kept, given = levels_of(me, arrived[2], ups, total)
    sums = pair_sums(kept, swap(given))
    sums = send_y(sums)
    new_w, new_m, new_v = adam(loss_row, sums, up_shard[0], moment_one[0], moment_two[0])
    shards = send_y(new_w)
    full = assemble(me, shards, swap(shards))

    back = {p: send_x(returned[p], -1) for p in (4, 3, 2, 0)}
    top, low, whole = (0, half), (half, half), (0, TOK)
    u, d = combine(hot[4], back[4], [0], [[]], split=2)
    u, d = send_z(u, d)
    u, d = combine(hot[3], back[3], [1, 0], [[(u, top)], [(d, low)]])
    u, d = send_z(u, d)
    u, d = combine(hot[2], back[2], [1, 0], [[(u, whole)], [(d, whole)]])
    u, d = send_z(u, d)
    u, d = combine(hot[0], back[0], [2, 1], [[(u, whole)], [(d, whole)]])
    u, d = send_z(u, d)
    (grad_tokens,) = combine(hot[0], back[0], [0], [[(u, whole), (d, whole)]], last=True)
    return (grad_tokens, full, new_m[None], new_v[None])


def solution(mesh):
    fine = Mesh(mesh.devices.reshape(NX, NZ, NY, 2), ("x", "z", "y", "core"))
    expert = ("x", "z")
    in_specs = (
        P(("x", "z", "y", "core"), None),
        P(("x", "z", "y", "core"), None),
        P(expert, ("y", "core"), None),
        P(expert, ("y", "core"), None),
        P(expert, ("y", "core"), None),
        P(expert, ("y", "core"), None),
        P(expert, ("y", "core"), None),
        P(),
    )
    out_specs = (
        P(("x", "z", "y", "core"), None),
        P(expert, None, None),
        P(expert, ("y", "core"), None),
        P(expert, ("y", "core"), None),
    )
    return jax.shard_map(step, mesh=fine, in_specs=in_specs, out_specs=out_specs, check_vma=False)
```
